512 devices in a mesh: sim: 64 (over z, y), lens: 8 (over x, core).
Axes of the slice: x: 4, y: 4, z: 16, core: 2. Of those that a mesh axis runs over, the one named last changes fastest.
Arguments:
- patches: bfloat16 [65536, 2, 2048], P(('sim', 'lens')), may hold values from -6 to 6
- patch_cycle: int32 [65536, 1], P(('sim', 'lens')), may hold values from 0 to 63; in each aligned block of 128 rows (0 to 127, 128 to 255, ...) at most 4 rows name the same one
- patch_block: int32 [65536], P(('sim', 'lens')), may hold values from 0 to 7
- m_values: int32 [128], replicated, may hold values from 0 to 8191, as said below
- shell_weight: float32 [2], replicated, may hold values from 0.5 to 2
- legendre_panel: bfloat16 [128, 512, 8192], P('sim', 'lens'), as said below
- spin2_panel: bfloat16 [128, 512, 8192], P('sim', 'lens'), as said below
Outputs:
- kappa_modes: float32 [128, 2, 512], P('sim', None, 'lens')
- shear_modes: float32 [128, 2, 512], P('sim', None, 'lens')
The draws below stay inside these ranges and needn't reach their ends.
Inputs may be any that keep to these rules, and one draw needn't show every extreme that they name: `patch_cycle`: among the 128 patches of one device, at most 4 lie on one cycle; some device reaches 4. `m_values`: the 128 orders are distinct; slots 2 d and 2 d + 1 hold m and 8191 - m with m below 4096, and some sim index holds 0 and 8191. legendre_panel[j, g, l] is 0 for l < 128 * (m_values[j] // 128). spin2_panel[j, g, l] is 0 for l < 128 * (m_values[j] // 128).
All inputs are finite; a program needn't handle non-finite values.
Results may differ from the reference program's by a relative error of at most 0.014.
Values may be sent and summed in bfloat16 or wider, within the bound.
A program may use at most 64 MiB of HBM per device.

```python
import math
import jax
import jax.numpy as jnp
import numpy as np
from jax import lax

NPIX = 16384
BPX = 2048
LMAX = 8192
LB = 128
SHELLS = 2
K_DEV = 128
NBLK = 8
CAP = 4
MW = 128
CYCLES = 512
PATCHES = 65536
N_SIM = 64
N_LENS = 8


def order_table(key):
    half = LMAX // 2
    others = jax.random.permutation(jax.random.fold_in(key, 7), half - 1)[:N_SIM - 1] + 1
    small = jnp.concatenate([jnp.array([0], jnp.int32), others.astype(jnp.int32)])
    small = jax.random.permutation(jax.random.fold_in(key, 8), small)
    pairs = jnp.stack([small, LMAX - 1 - small], axis=1)
    return pairs.reshape(-1).astype(jnp.int32)


def panel_values(key, salt):
    orders = order_table(key)
    ell = jnp.arange(LMAX, dtype=jnp.int32)
    keep = (ell[None, :] >= LB * (orders // LB)[:, None]).astype(jnp.float32)
    inner_key = jax.random.fold_in(key, salt)
    values = jax.random.normal(inner_key, (MW, CYCLES, LMAX), jnp.float32)
    return (values * keep[:, None, :]).astype(jnp.bfloat16)


def draw_m_values(key, part):
    return order_table(key)


def draw_legendre_panel(key, part):
    return panel_values(key, 21)


def draw_spin2_panel(key, part):
    return panel_values(key, 22)


def touch_ends(result, rng, low, high):
    longest = result.shape.index(max(result.shape))
    spots = []
    for shift in (0, 1):
        where = [jax.random.randint(jax.random.fold_in(rng, axis), (), 0, length) for axis, length in enumerate(result.shape)]
        where[longest] = (where[longest] + shift) % result.shape[longest]
        spots.append(tuple(where))
    return result.at[spots[0]].set(low).at[spots[1]].set(high)


def block_scale(stream_key, dims, pieces, least, top_value):
    def one(position, blocks):
        draws = jax.random.uniform(jax.random.fold_in(jax.random.fold_in(stream_key, 6), position), (blocks,), jnp.float32, least / len(pieces), top_value / len(pieces))
        return jnp.repeat(jnp.exp(draws), dims[position] // blocks).reshape((-1,) + (1,) * (len(dims) - position - 1))

    factor_of = one(*pieces[0])
    for cut in pieces[1:]:
        factor_of = factor_of * one(*cut)
    return factor_of


def shared_out(own_key, own, number, rows, count, top, most, slope):
    sequence = jax.random.permutation(own_key, count)
    crowded, usual = portions_of(count, rows * top, most, slope, True), portions_of(count, rows * top, most, slope, False)
    places = jnp.arange(count)

    def named(sizes, offset_by):
        used = int((sizes > 0).sum())
        fixed = max(1, used // 4)
        moved = fixed + (places - fixed + offset_by * (used - fixed)) % max(1, count - fixed)
        return jnp.zeros((count,), jnp.int32).at[sequence[jnp.where(places < fixed, places, moved)]].set(jnp.asarray(sizes, jnp.int32))

    sizes = jnp.where(number % 4 == 0, named(crowded, number // 4), named(usual, number - number // 4 - 1))
    mixed = jax.random.permutation(jax.random.fold_in(own, 3), count)
    donor, sink = mixed[0:count // 2 * 2:2], mixed[1:count // 2 * 2:2]
    room = jnp.minimum(sizes[donor] - 1, most - sizes[sink]) // 2
    room = jnp.where((donor == sequence[0]) | (sink == sequence[0]) | (sizes[sink] == 0), 0, jnp.maximum(room, 0))
    moved = jax.random.randint(jax.random.fold_in(own, 4), (count // 2,), 0, 1 << 20) % (room + 1)
    sizes = sizes.at[donor].add(-moved).at[sink].add(moved)
    labels = jnp.searchsorted(jnp.cumsum(sizes), jnp.arange(rows * top), side="right").astype(jnp.int32)
    listing = labels.reshape(top, rows).T
    listing = listing[jax.random.permutation(jax.random.fold_in(own, 1), rows)]
    offset_by = jax.random.randint(jax.random.fold_in(own, 2), (rows, 1), 0, top)
    return jnp.take_along_axis(listing, (jnp.arange(top)[None, :] + offset_by) % top, axis=1)


def portions_of(number_of, total, limit, slope, full):
    loads = [(1 << 20) // math.isqrt(grade ** slope) + 1 for grade in range(1, number_of + 1)]
    largest = limit if full else min(limit, max(-(-total // number_of), total * loads[0] // sum(loads)))
    least = 1 if total - largest >= number_of - 1 else 0
    holding, rest = [largest] + [least] * (number_of - 1), total - largest - least * (number_of - 1)
    while rest > 0:
        free = [i for i in range(1, number_of) if holding[i] < largest] or [i for i in range(1, number_of) if holding[i] < limit]
        pool, remaining = sum([loads[i] for i in free]), rest
        for i in free:
            more = min(limit - holding[i], max(1, remaining * loads[i] // pool), rest)
            holding[i] = holding[i] + more
            rest = rest - more
    return np.array(holding)


def centred(key, dims, spread, limit, cuts=(), held_as=jnp.bfloat16):
    values = spread * jax.random.normal(key, dims, jnp.float32)
    if cuts:
        values = values * block_scale(key, dims, cuts, -0.22, 0.18)
    return jnp.clip(values, -limit, limit).astype(held_as)


def setup_inputs(seed: int = 0) -> dict:
    key_list = jax.random.split(jax.random.key(seed), 8)
    patches = centred(key_list[0], (PATCHES, SHELLS, BPX), 1.0, 6.0, ((0, 512),))
    patch_cycle_keys = jax.random.split(jax.random.fold_in(key_list[1], 1), PATCHES // K_DEV)
    patch_cycle_turns = jax.random.permutation(jax.random.fold_in(key_list[1], 3), PATCHES // K_DEV)
    patch_cycle = jax.vmap(lambda own, number: shared_out(jax.random.fold_in(key_list[1], 2), own, number, K_DEV, N_SIM, 1, CAP, 2))(patch_cycle_keys, patch_cycle_turns).reshape((PATCHES, 1))
    patch_block = touch_ends(jax.random.randint(key_list[2], (PATCHES,), 0, NBLK), jax.random.fold_in(key_list[2], 1), 0, NBLK - 1).astype(jnp.int32)
    m_values = draw_m_values(jax.random.fold_in(key_list[7], 71), 0)
    shell_weight = jnp.clip(jnp.exp(jax.random.uniform(key_list[4], (SHELLS,), jnp.float32, math.log(0.5), math.log(2.0))), 0.5, 2.0)
    legendre_panel = draw_legendre_panel(jax.random.fold_in(key_list[7], 71), 0)
    spin2_panel = draw_spin2_panel(jax.random.fold_in(key_list[7], 71), 0)
    return {"patches": patches, "patch_cycle": patch_cycle, "patch_block": patch_block, "m_values": m_values, "shell_weight": shell_weight, "legendre_panel": legendre_panel, "spin2_panel": spin2_panel}


def cycle_table(m_values, parity):
    pixel = jnp.arange(NPIX, dtype=jnp.int32)
    angle_index = (2 * pixel[:, None] * m_values[None, :] + parity * m_values[None, :]) % (2 * NPIX)
    angle = angle_index.astype(jnp.float32) * (math.pi / NPIX)
    return jnp.concatenate([jnp.cos(angle), jnp.sin(angle)], axis=1)

def reference(patches, patch_cycle, patch_block, m_values, shell_weight, legendre_panel, spin2_panel):
    cycles = N_SIM * N_LENS
    device = jnp.arange(K_DEV * N_SIM * N_LENS, dtype=jnp.int32) // K_DEV
    column = device % N_LENS
    cycle_global = column * N_SIM + patch_cycle[:, 0]
    segment = cycle_global * NBLK + patch_block
    density = jax.ops.segment_sum(patches.astype(jnp.float32), segment, num_segments=cycles * NBLK)
    density = density.reshape(cycles, NBLK, SHELLS, BPX).transpose(0, 2, 1, 3).reshape(cycles, SHELLS, NPIX)
    halves = []
    for parity in range(2):
        rows = density[parity::2].reshape(-1, NPIX)
        sums = jnp.dot(rows, cycle_table(m_values, parity), precision=lax.Precision.HIGHEST)
        halves.append(sums.reshape(cycles // 2, SHELLS, 2, MW))
    sums = jnp.stack(halves, axis=1).reshape(cycles, SHELLS, 2, MW)
    modes = jnp.stack([sums[:, :, 0], -sums[:, :, 1]], axis=2) / math.sqrt(NPIX)
    modes_rounded = modes.astype(jnp.bfloat16).reshape(cycles, SHELLS * 2, MW).transpose(2, 0, 1)

    def analyse(items):
        panel, coeffs = items
        return jnp.dot(coeffs.T, panel, preferred_element_type=jnp.float32)
    delta = lax.map(analyse, (legendre_panel, modes_rounded)).reshape(MW, SHELLS, 2, LMAX)
    kappa = jnp.zeros((MW, 2, LMAX), jnp.float32)
    for shell in range(SHELLS):
        kappa = kappa + shell_weight[shell] * delta[:, shell]
    kappa = kappa / math.sqrt(cycles)
    ell = jnp.arange(LMAX, dtype=jnp.int32).astype(jnp.float32)
    factor = jnp.where(ell >= 2.0, jnp.sqrt((ell + 2.0) * (ell - 1.0) / jnp.maximum(ell * (ell + 1.0), 1.0)), 0.0)
    shear = kappa * factor
    kappa_rounded = kappa.astype(jnp.bfloat16)
    shear_rounded = shear.astype(jnp.bfloat16)

    def synthesise(items):
        spin_zero, spin_two, kappa_row, shear_row = items
        return (jnp.dot(kappa_row, spin_zero.T, preferred_element_type=jnp.float32), jnp.dot(shear_row, spin_two.T, preferred_element_type=jnp.float32))
    kappa_modes, shear_modes = lax.map(synthesise, (legendre_panel, spin2_panel, kappa_rounded, shear_rounded))
    scale = 1.0 / math.sqrt(LMAX)
    return (kappa_modes * scale, shear_modes * scale)
```

```python
import math

import jax
import jax.numpy as jnp
from jax import lax
from jax.experimental import pallas as pl
from jax.experimental.pallas import tpu as pltpu
from jax.sharding import PartitionSpec as P

NPIX = 16384
BPX = 2048
LMAX = 8192
SHELLS = 2
NZ = 16
NY = 4
NLENS = 8
K_DEV = 128
ROWS = K_DEV * SHELLS
LCHUNK = LMAX // NLENS
MESH = pl.DeviceIdType.MESH
F32 = jnp.float32
BF16 = jnp.bfloat16


def split(value):
    high = value.astype(BF16)
    return high, (value - high.astype(F32)).astype(BF16)


def mxu(a, b):
    return jnp.dot(a, b, preferred_element_type=F32)


def cos_sin(index):
    quarter = (index + 4096) >> 13
    t = (index - (quarter << 13)).astype(F32) * (2.0 * math.pi / 32768)
    t2 = t * t
    c = 1.0 + t2 * (-0.5 + t2 * (1 / 24 + t2 * (-1 / 720 + t2 * (1 / 40320))))
    s = t * (1.0 + t2 * (-1 / 6 + t2 * (1 / 120 + t2 * (-1 / 5040 + t2 * (1 / 362880)))))
    odd = (quarter & 1) == 1
    cosine = jnp.where(odd, s, c)
    sine = jnp.where(odd, c, s)
    cosine = jnp.where(((quarter + 1) & 2) == 2, -cosine, cosine)
    sine = jnp.where((quarter & 2) == 2, -sine, sine)
    return cosine, sine


def iota(shape, dim):
    return lax.broadcasted_iota(jnp.int32, shape, dim)


def kernel(
    cycle_hbm, block_hbm, m_hbm, weight, x_hbm, l_hbm, s_hbm,
    kappa_out, shear_out,
    small, xv, lv, sv, table_hi, table_lo, base, turn, factor,
    part, recv_y, summed, recv_z, kpart, recv_k, kfull,
    small_sem, x_sem, panel_sem,
    send_y, got_y, send_z, got_z, send_k, got_k, send_g, got_g,
):
    sim = lax.axis_index("sim")
    lens = lax.axis_index("lens")
    z = sim // NY
    y = sim % NY

    def sim_id(z_to, y_to):
        return (z_to * NY + y_to, lens)

    barrier = pltpu.get_barrier_semaphore()
    for d in range(1, NZ):
        pl.semaphore_signal(
            barrier, inc=1, device_id=sim_id((z + d) % NZ, y), device_id_type=MESH
        )
    for d in range(1, NY):
        pl.semaphore_signal(
            barrier, inc=1, device_id=sim_id(z, (y + d) % NY), device_id_type=MESH
        )
    for d in range(1, NLENS):
        pl.semaphore_signal(
            barrier, inc=1, device_id=(sim, (lens + d) % NLENS), device_id_type=MESH
        )

    small_copies = [
        pltpu.make_async_copy(source, small.at[i], small_sem.at[i])
        for i, source in enumerate((cycle_hbm, block_hbm, m_hbm))
    ]
    for copy in small_copies:
        copy.start()
    x_copies = [
        pltpu.make_async_copy(
            x_hbm.at[:, :, pl.ds(512 * i, 512)], xv.at[:, :, pl.ds(512 * i, 512)], x_sem.at[i]
        )
        for i in range(4)
    ]
    for copy in x_copies:
        copy.start()
    l_copy = pltpu.make_async_copy(l_hbm, lv, panel_sem.at[0])
    s_copy = pltpu.make_async_copy(s_hbm, sv, panel_sem.at[1])
    l_copy.start()
    s_copy.start()
    for copy in small_copies:
        copy.wait()

    cycle_row = small[0]
    block_row = small[1]
    m_row = jnp.broadcast_to(small[2], (8, 128))
    row = iota((128, 128), 0)
    column = iota((128, 128), 1)
    slot = 8 * (column & 15) + 2 * ((column >> 4) & 3) + (column >> 6)
    permute = (row == slot).astype(BF16)
    m_high = mxu((m_row >> 6).astype(F32).astype(BF16), permute)
    m_low = mxu((m_row & 63).astype(F32).astype(BF16), permute)
    orders = (m_high * 64.0 + m_low).astype(jnp.int32)[0:1]

    a_cos, a_sin = cos_sin((128 * iota((32, 128), 0) * orders) & 32767)
    base[0, 0:32] = a_cos
    base[1, 0:32] = a_sin
    b_cos, b_sin = cos_sin((2 * iota((64, 128), 0) * orders) & 32767)

    def fill(a, carry):
        ca = base[0, pl.ds(a, 1), :]
        sa = base[1, pl.ds(a, 1), :]
        rows = pl.ds(pl.multiple_of(a * 64, 64), 64)
        c_high, c_low = split(ca * b_cos - sa * b_sin)
        s_high, s_low = split(sa * b_cos + ca * b_sin)
        table_hi[rows, 0:128] = c_high
        table_hi[rows, 128:256] = s_high
        table_lo[rows, 0:128] = c_low
        table_lo[rows, 128:256] = s_low
        return carry

    lax.fori_loop(0, 32, fill, 0)

    code = (block_row * 64 + cycle_row).astype(F32)
    row2 = iota((ROWS, 128), 0)
    picked = jnp.where(iota((ROWS, 128), 1) == (row2 >> 1), code, 0.0)
    code_column = jnp.sum(picked, axis=1, keepdims=True).astype(jnp.int32)
    phase = (code_column >> 6) * (2 * BPX) + (code_column & 1)
    turn_cos, turn_sin = cos_sin((phase * orders) & 32767)
    scale = 1.0 / (math.sqrt(NPIX) * math.sqrt(NZ * NY * NLENS))
    row_weight = jnp.where((row2 & 1) == 0, weight[0], weight[1]) * scale
    turn[0] = turn_cos * row_weight
    turn[1] = turn_sin * row_weight
    spread = (iota((128, ROWS), 0) == (iota((128, ROWS), 1) >> 1)).astype(BF16)
    cycle_wide = mxu(
        jnp.broadcast_to(cycle_row, (8, 128)).astype(F32).astype(BF16), spread
    )[0:1]
    onehot = ((iota((128, ROWS), 0) & 63).astype(F32) == cycle_wide).astype(F32).astype(BF16)

    ell = (LCHUNK * iota((8, LCHUNK), 0) + iota((8, LCHUNK), 1)).astype(F32)
    factor[...] = jnp.where(
        ell >= 2.0,
        jnp.sqrt((ell + 2.0) * (ell - 1.0) / jnp.maximum(ell * (ell + 1.0), 1.0)),
        0.0,
    )

    total = jnp.zeros((ROWS, 256), F32)
    for i in range(8):
        if i % 2 == 0:
            x_copies[i // 2].wait()
        piece = xv[:, :, 256 * i : 256 * i + 256].reshape(ROWS, 256)
        total = total + mxu(piece, table_hi[256 * i : 256 * i + 256])
        total = total + mxu(piece, table_lo[256 * i : 256 * i + 256])
    zc = total[:, 0:128]
    zs = total[:, 128:256]
    real = turn[0] * zc - turn[1] * zs
    imag = -(turn[1] * zc + turn[0] * zs)
    high, low = split(jnp.concatenate([real, imag], axis=1))
    gathered = mxu(onehot, high) + mxu(onehot, low)
    left = iota((64, 128), 1) < 64
    for c in range(2):
        turned = gathered[:, 128 * c : 128 * c + 128].T
        part[:, c, :] = jnp.where(left, turned[0:64], turned[64:128])

    pl.semaphore_wait(barrier, NZ - 1 + NY - 1 + NLENS - 1)

    copies = []
    for d in range(1, NY):
        y_to = (y + d) % NY
        copy = pltpu.make_async_remote_copy(
            src_ref=part.at[pl.ds(y_to * NZ, NZ)],
            dst_ref=recv_y.at[d - 1],
            send_sem=send_y.at[d - 1],
            recv_sem=got_y.at[d - 1],
            device_id=sim_id(z, y_to),
            device_id_type=MESH,
        )
        copy.start()
        copies.append(copy)
    for copy in copies:
        copy.wait_recv()
    summed[...] = part[pl.ds(y * NZ, NZ)] + recv_y[0] + (recv_y[1] + recv_y[2])
    for d in range(1, NZ):
        z_to = (z + d) % NZ
        copy = pltpu.make_async_remote_copy(
            src_ref=summed.at[z_to],
            dst_ref=recv_z.at[d - 1],
            send_sem=send_z.at[d - 1],
            recv_sem=got_z.at[d - 1],
            device_id=sim_id(z_to, y),
            device_id_type=MESH,
        )
        copy.start()
        copies.append(copy)
    l_copy.wait()
    s_copy.wait()
    for copy in copies[NY - 1 :]:
        copy.wait_recv()
    modes = summed[z]
    for d in range(NZ - 1):
        modes = modes + recv_z[d]

    side = iota((2, 128), 1) < 64
    rows4 = jnp.concatenate(
        [
            jnp.where(side, modes, 0.0),
            jnp.where(side, 0.0, modes),
            jnp.zeros((4, 128), F32),
        ],
        axis=0,
    ).astype(BF16)
    for i in range(NLENS):
        columns = slice(LCHUNK * i, LCHUNK * (i + 1))
        kappa = mxu(rows4, lv[:, :, columns].reshape(128, LCHUNK))
        kpart[i] = kappa[0:4].astype(BF16)

    copies_k = []
    for d in range(1, NLENS):
        lens_to = (lens + d) % NLENS
        copy = pltpu.make_async_remote_copy(
            src_ref=kpart.at[lens_to],
            dst_ref=recv_k.at[d - 1],
            send_sem=send_k.at[d - 1],
            recv_sem=got_k.at[d - 1],
            device_id=(sim, lens_to),
            device_id_type=MESH,
        )
        copy.start()
        copies_k.append(copy)
    for copy in copies_k:
        copy.wait_recv()
    kappa = kpart[lens].astype(F32)
    for d in range(NLENS - 1):
        kappa = kappa + recv_k[d].astype(F32)
    kfull[lens] = kappa.astype(BF16)
    copies_g = []
    for d in range(1, NLENS):
        lens_to = (lens + d) % NLENS
        copy = pltpu.make_async_remote_copy(
            src_ref=kfull.at[lens],
            dst_ref=kfull.at[lens],
            send_sem=send_g.at[d - 1],
            recv_sem=got_g.at[d - 1],
            device_id=(sim, lens_to),
            device_id_type=MESH,
        )
        copy.start()
        copies_g.append(copy)
    for copy in copies_g:
        copy.wait_recv()

    pad = jnp.zeros((4, LCHUNK), F32)
    out_k = jnp.zeros((8, 128), F32)
    out_s = jnp.zeros((8, 128), F32)
    contract = (((1,), (1,)), ((), ()))
    for i in range(NLENS):
        columns = slice(LCHUNK * i, LCHUNK * (i + 1))
        kappa = jnp.concatenate([kfull[i].astype(F32), pad], axis=0)
        shear = kappa * factor[i : i + 1, :]
        out_k = out_k + lax.dot_general(
            kappa.astype(BF16),
            lv[:, :, columns].reshape(128, LCHUNK),
            contract,
            preferred_element_type=F32,
        )
        out_s = out_s + lax.dot_general(
            shear.astype(BF16),
            sv[:, :, columns].reshape(128, LCHUNK),
            contract,
            preferred_element_type=F32,
        )
    scale = 1.0 / math.sqrt(LMAX)
    for b in range(2):
        kappa_out[b] = out_k[2 * b : 2 * b + 2, 64 * b : 64 * b + 64] * scale
        shear_out[b] = out_s[2 * b : 2 * b + 2, 64 * b : 64 * b + 64] * scale
    for copy in copies + copies_k + copies_g:
        copy.wait_send()


def on_device(
    patches, patch_cycle, patch_block, m_values, shell_weight, legendre_panel, spin2_panel
):
    hbm = pl.BlockSpec(memory_space=pl.ANY)
    vmem = pl.BlockSpec(memory_space=pltpu.VMEM)
    shape = jax.ShapeDtypeStruct((2, 2, 64), F32)
    dma = pltpu.SemaphoreType.DMA
    return pl.pallas_call(
        kernel,
        out_shape=(shape, shape),
        in_specs=[hbm, hbm, hbm, pl.BlockSpec(memory_space=pltpu.SMEM), hbm, hbm, hbm],
        out_specs=(vmem, vmem),
        scratch_shapes=[
            pltpu.VMEM((3, 1, 128), jnp.int32),
            pltpu.VMEM((K_DEV, SHELLS, BPX), BF16),
            pltpu.VMEM((2, 64, LMAX), BF16),
            pltpu.VMEM((2, 64, LMAX), BF16),
            pltpu.VMEM((BPX, 256), BF16),
            pltpu.VMEM((BPX, 256), BF16),
            pltpu.VMEM((2, 32, 128), F32),
            pltpu.VMEM((2, ROWS, 128), F32),
            pltpu.VMEM((8, LCHUNK), F32),
            pltpu.VMEM((NY * NZ, 2, 128), F32),
            pltpu.VMEM((NY - 1, NZ, 2, 128), F32),
            pltpu.VMEM((NZ, 2, 128), F32),
            pltpu.VMEM((NZ - 1, 2, 128), F32),
            pltpu.VMEM((NLENS, 4, LCHUNK), BF16),
            pltpu.VMEM((NLENS - 1, 4, LCHUNK), BF16),
            pltpu.VMEM((NLENS, 4, LCHUNK), BF16),
            dma((3,)),
            dma((4,)),
            dma((2,)),
            dma((NY - 1,)),
            dma((NY - 1,)),
            dma((NZ - 1,)),
            dma((NZ - 1,)),
            dma((NLENS - 1,)),
            dma((NLENS - 1,)),
            dma((NLENS - 1,)),
            dma((NLENS - 1,)),
        ],
        compiler_params=pltpu.CompilerParams(collective_id=0, has_side_effects=True),
        name="shear_step",
    )(
        patch_cycle.reshape(1, K_DEV),
        patch_block.reshape(1, K_DEV),
        m_values.reshape(1, 128),
        shell_weight,
        patches,
        legendre_panel,
        spin2_panel,
    )


def solution(mesh):
    placed = (
        P(("sim", "lens"), None, None),
        P(("sim", "lens"), None),
        P(("sim", "lens")),
        P(),
        P(),
        P("sim", "lens", None),
        P("sim", "lens", None),
    )
    return jax.shard_map(
        on_device,
        mesh=mesh,
        in_specs=placed,
        out_specs=(P("sim", None, "lens"), P("sim", None, "lens")),
        check_vma=False,
    )
```

```python
import math

import jax
import jax.numpy as jnp
from jax import lax
from jax.experimental import pallas as pl
from jax.experimental.pallas import tpu as pltpu
from jax.sharding import PartitionSpec as P

NPIX = 16384
BPX = 2048
LMAX = 8192
SHELLS = 2
NZ = 16
NY = 4
NLENS = 8
K_DEV = 128
ROWS = K_DEV * SHELLS
BLOCK = 128
HALF = 33
WIDE = HALF * BLOCK
CHUNKS = ((0, 12), (12, 24), (24, 33))
NEAR = 4
MESH = pl.DeviceIdType.MESH
F32 = jnp.float32
BF16 = jnp.bfloat16


def split(value):
    high = value.astype(BF16)
    return high, (value - high.astype(F32)).astype(BF16)


def mxu(a, b):
    return jnp.dot(a, b, preferred_element_type=F32)


def cos_sin(index):
    quarter = (index + 4096) >> 13
    t = (index - (quarter << 13)).astype(F32) * (2.0 * math.pi / 32768)
    t2 = t * t
    c = 1.0 + t2 * (-0.5 + t2 * (1 / 24 + t2 * (-1 / 720 + t2 * (1 / 40320))))
    s = t * (1.0 + t2 * (-1 / 6 + t2 * (1 / 120 + t2 * (-1 / 5040 + t2 * (1 / 362880)))))
    odd = (quarter & 1) == 1
    cosine = jnp.where(odd, s, c)
    sine = jnp.where(odd, c, s)
    cosine = jnp.where(((quarter + 1) & 2) == 2, -cosine, cosine)
    sine = jnp.where((quarter & 2) == 2, -sine, sine)
    return cosine, sine


def iota(shape, dim):
    return lax.broadcasted_iota(jnp.int32, shape, dim)


def kernel(
    cycle_hbm, block_hbm, m_hbm, weight, x_hbm, l_hbm, s_hbm,
    raw,
    small, xv, lv, sv, lc, sc, table_hi, table_lo, base, turn, factor,
    part, recv_y, summed, recv_z, kpart, recv_k,
    small_sem, x_sem, panel_sem, far,
    send_y, got_y, send_z, got_z, send_k, got_k,
):
    sim = lax.axis_index("sim")
    lens = lax.axis_index("lens")
    z = sim // NY
    y = sim % NY

    def sim_id(z_to, y_to):
        return (z_to * NY + y_to, lens)

    barrier = pltpu.get_barrier_semaphore()
    near = [d for d in range(1, NZ) if min(d, NZ - d) <= NEAR]
    for d in near:
        pl.semaphore_signal(
            barrier, inc=1, device_id=sim_id((z + d) % NZ, y), device_id_type=MESH
        )
    for d in range(1, NY):
        pl.semaphore_signal(
            barrier, inc=1, device_id=sim_id(z, (y + d) % NY), device_id_type=MESH
        )
    for d in range(1, NLENS):
        pl.semaphore_signal(
            barrier, inc=1, device_id=(sim, (lens + d) % NLENS), device_id_type=MESH
        )

    small_copies = [
        pltpu.make_async_copy(source, small.at[i], small_sem.at[i])
        for i, source in enumerate((cycle_hbm, block_hbm, m_hbm))
    ]
    for copy in small_copies:
        copy.start()
    x_copies = [
        pltpu.make_async_copy(
            x_hbm.at[:, :, pl.ds(512 * i, 512)], xv.at[:, :, pl.ds(512 * i, 512)], x_sem.at[i]
        )
        for i in range(4)
    ]
    for copy in x_copies:
        copy.start()
    l_copy = pltpu.make_async_copy(l_hbm, lv, panel_sem.at[0])
    s_copy = pltpu.make_async_copy(s_hbm, sv, panel_sem.at[1])
    for copy in small_copies:
        copy.wait()

    cycle_row = small[0]
    block_row = small[1]
    m_row = jnp.broadcast_to(small[2], (8, 128))
    row = iota((128, 128), 0)
    column = iota((128, 128), 1)
    slot = 8 * (column & 15) + 2 * ((column >> 4) & 3) + (column >> 6)
    permute = (row == slot).astype(BF16)
    m_high = mxu((m_row >> 6).astype(F32).astype(BF16), permute)
    m_low = mxu((m_row & 63).astype(F32).astype(BF16), permute)
    orders = (m_high * 64.0 + m_low).astype(jnp.int32)[0:1]

    a_cos, a_sin = cos_sin((128 * iota((32, 128), 0) * orders) & 32767)
    base[0, 0:32] = a_cos
    base[1, 0:32] = a_sin
    b_cos, b_sin = cos_sin((2 * iota((64, 128), 0) * orders) & 32767)

    def fill(a, carry):
        ca = base[0, pl.ds(a, 1), :]
        sa = base[1, pl.ds(a, 1), :]
        rows = pl.ds(pl.multiple_of(a * 64, 64), 64)
        c_high, c_low = split(ca * b_cos - sa * b_sin)
        s_high, s_low = split(sa * b_cos + ca * b_sin)
        table_hi[rows, 0:128] = c_high
        table_hi[rows, 128:256] = s_high
        table_lo[rows, 0:128] = c_low
        table_lo[rows, 128:256] = s_low
        return carry

    lax.fori_loop(0, 32, fill, 0)

    code = (block_row * 64 + cycle_row).astype(F32)
    row2 = iota((ROWS, 128), 0)
    picked = jnp.where(iota((ROWS, 128), 1) == (row2 >> 1), code, 0.0)
    code_column = jnp.sum(picked, axis=1, keepdims=True).astype(jnp.int32)
    phase = (code_column >> 6) * (2 * BPX) + (code_column & 1)
    turn_cos, turn_sin = cos_sin((phase * orders) & 32767)
    scale = 1.0 / (math.sqrt(NPIX) * math.sqrt(NZ * NY * NLENS))
    row_weight = jnp.where((row2 & 1) == 0, weight[0], weight[1]) * scale
    turn[0] = turn_cos * row_weight
    turn[1] = turn_sin * row_weight
    spread = (iota((128, ROWS), 0) == (iota((128, ROWS), 1) >> 1)).astype(BF16)
    cycle_wide = mxu(
        jnp.broadcast_to(cycle_row, (8, 128)).astype(F32).astype(BF16), spread
    )[0:1]
    onehot = ((iota((128, ROWS), 0) & 63).astype(F32) == cycle_wide).astype(F32).astype(BF16)

    total = jnp.zeros((ROWS, 256), F32)
    for i in range(8):
        if i % 2 == 0:
            x_copies[i // 2].wait()
        piece = xv[:, :, 256 * i : 256 * i + 256].reshape(ROWS, 256)
        total = total + mxu(piece, table_hi[256 * i : 256 * i + 256])
        total = total + mxu(piece, table_lo[256 * i : 256 * i + 256])
    l_copy.start()
    s_copy.start()
    zc = total[:, 0:128]
    zs = total[:, 128:256]
    real = turn[0] * zc - turn[1] * zs
    imag = -(turn[1] * zc + turn[0] * zs)
    high, low = split(jnp.concatenate([real, imag], axis=1))
    gathered = mxu(onehot, high) + mxu(onehot, low)
    left = iota((64, 128), 1) < 64
    for c in range(2):
        turned = gathered[:, 128 * c : 128 * c + 128].T
        part[:, c, :] = jnp.where(left, turned[0:64], turned[64:128])

    pl.semaphore_wait(barrier, len(near) + NY - 1 + NLENS - 1)
    for d in (NEAR, NZ - NEAR):
        pl.semaphore_signal(far, inc=1, device_id=sim_id((z + d) % NZ, y), device_id_type=MESH)

    copies = []
    for d in range(1, NY):
        y_to = (y + d) % NY
        copy = pltpu.make_async_remote_copy(
            src_ref=part.at[pl.ds(y_to * NZ, NZ)],
            dst_ref=recv_y.at[d - 1],
            send_sem=send_y.at[d - 1],
            recv_sem=got_y.at[d - 1],
            device_id=sim_id(z, y_to),
            device_id_type=MESH,
        )
        copy.start()
        copies.append(copy)

    own_order = jnp.where(iota((8, 128), 1) == 2 * sim, m_row, 0)
    first = jnp.sum((own_order >> 7).astype(F32), axis=1, keepdims=True)[0:1]
    first16 = jnp.broadcast_to(first, (16, 128))
    below = [jnp.clip(first16 - p, 0.0, 1.0) for p in range(-1, 64)]
    for copy, panel, compact in ((l_copy, lv, lc), (s_copy, sv, sc)):
        copy.wait()
        for r in range(0, 64, 16):
            last = jnp.zeros((16, BLOCK), BF16)
            for p in range(64):
                up, at = divmod(p, HALF)
                one = panel[0, r : r + 16, BLOCK * p : BLOCK * p + BLOCK]
                two = panel[1, r : r + 16, BLOCK * (63 - p) : BLOCK * (64 - p)]
                mixed = one * (1.0 - below[p + 1]).astype(BF16) + two * below[p + 1].astype(BF16)
                last = last + two * (below[p] - below[p + 1]).astype(BF16)
                compact[64 * up + r : 64 * up + r + 16, BLOCK * at : BLOCK * at + BLOCK] = mixed
            compact[64 + r : 64 + r + 16, WIDE - 2 * BLOCK : WIDE - BLOCK] = last
            compact[64 + r : 64 + r + 16, WIDE - BLOCK : WIDE] = jnp.zeros((16, BLOCK), BF16)
    first = jnp.broadcast_to(first, (4, WIDE)).astype(jnp.int32)
    position = (iota((4, WIDE), 1) >> 7) + HALF * (iota((4, WIDE), 0) >> 1)
    second = (position < first) | (position >= 64)
    block = jnp.where(position < first, 63 - position, jnp.where(position >= 64, 63 - first, position))
    ell = (BLOCK * block + (iota((4, WIDE), 1) & 127)).astype(F32)
    factor[...] = jnp.where(
        ell >= 2.0,
        jnp.sqrt((ell + 2.0) * (ell - 1.0) / jnp.maximum(ell * (ell + 1.0), 1.0)),
        0.0,
    )

    for copy in copies:
        copy.wait_recv()
    summed[...] = part[pl.ds(y * NZ, NZ)] + recv_y[0] + (recv_y[1] + recv_y[2])
    pl.semaphore_wait(far, 2)
    for d in range(1, NZ):
        z_to = (z + d) % NZ
        copy = pltpu.make_async_remote_copy(
            src_ref=summed.at[z_to],
            dst_ref=recv_z.at[d - 1],
            send_sem=send_z.at[d - 1],
            recv_sem=got_z.at[d - 1],
            device_id=sim_id(z_to, y),
            device_id_type=MESH,
        )
        copy.start()
        copies.append(copy)
    for copy in copies[NY - 1 :]:
        copy.wait_recv()
    modes = summed[z]
    for d in range(NZ - 1):
        modes = modes + recv_z[d]

    side = iota((2, 128), 1) < 64
    other = pltpu.roll(modes, 64, 1)
    rows8 = jnp.concatenate(
        [
            jnp.where(side, modes, 0.0),
            jnp.where(side, 0.0, other),
            jnp.where(side, other, 0.0),
            jnp.where(side, 0.0, modes),
        ],
        axis=0,
    ).astype(BF16)
    copies_k = []
    for i, (start, end) in enumerate(CHUNKS):
        lanes = slice(BLOCK * start, BLOCK * end)
        kappa = mxu(rows8, lc[:, lanes])
        kpart[:, lanes] = jnp.where(second[:, lanes], kappa[4:8], kappa[0:4]).astype(BF16)
        window = pl.ds(BLOCK * start, BLOCK * (end - start))
        for d in range(1, NLENS):
            lens_to = (lens + d) % NLENS
            copy = pltpu.make_async_remote_copy(
                src_ref=kpart.at[:, window],
                dst_ref=recv_k.at[d - 1, :, window],
                send_sem=send_k.at[d - 1, i],
                recv_sem=got_k.at[d - 1, i],
                device_id=(sim, lens_to),
                device_id_type=MESH,
            )
            copy.start()
            copies_k.append(copy)

    out_k = jnp.zeros((8, 128), F32)
    out_s = jnp.zeros((8, 128), F32)
    contract = (((1,), (1,)), ((), ()))
    for i, (start, end) in enumerate(CHUNKS):
        lanes = slice(BLOCK * start, BLOCK * end)
        kappa = kpart[:, lanes].astype(F32)
        for d in range(NLENS - 1):
            copies_k[(NLENS - 1) * i + d].wait_recv()
            kappa = kappa + recv_k[d, :, lanes].astype(F32)
        zero = jnp.zeros_like(kappa)
        of_second = second[:, lanes]
        shear = kappa * factor[:, lanes]
        for value, panel, kind in ((kappa, lc, 0), (shear, sc, 1)):
            value8 = jnp.concatenate(
                [jnp.where(of_second, zero, value), jnp.where(of_second, value, zero)], axis=0
            )
            out = lax.dot_general(
                value8.astype(BF16), panel[:, lanes], contract, preferred_element_type=F32
            )
            if kind == 0:
                out_k = out_k + out
            else:
                out_s = out_s + out
    scale = 1.0 / math.sqrt(LMAX)
    raw[0] = out_k * scale
    raw[1] = out_s * scale
    for copy in copies + copies_k:
        copy.wait_send()


def finish(raw, kappa_out, shear_out):
    for kind, out in ((0, kappa_out), (1, shear_out)):
        for b in range(2):
            out[b] = raw[kind, 4 * b : 4 * b + 2, 0:64] + raw[kind, 4 * b + 2 : 4 * b + 4, 64:128]


def on_device(
    patches, patch_cycle, patch_block, m_values, shell_weight, legendre_panel, spin2_panel
):
    hbm = pl.BlockSpec(memory_space=pl.ANY)
    vmem = pl.BlockSpec(memory_space=pltpu.VMEM)
    smem = pl.BlockSpec(memory_space=pltpu.SMEM)
    shape = jax.ShapeDtypeStruct((2, 2, 64), F32)
    dma = pltpu.SemaphoreType.DMA
    raw = pl.pallas_call(
        kernel,
        out_shape=jax.ShapeDtypeStruct((2, 8, 128), F32),
        in_specs=[hbm, hbm, hbm, smem, hbm, hbm, hbm],
        out_specs=vmem,
        scratch_shapes=[
            pltpu.VMEM((3, 1, 128), jnp.int32),
            pltpu.VMEM((K_DEV, SHELLS, BPX), BF16),
            pltpu.VMEM((2, 64, LMAX), BF16),
            pltpu.VMEM((2, 64, LMAX), BF16),
            pltpu.VMEM((128, WIDE), BF16),
            pltpu.VMEM((128, WIDE), BF16),
            pltpu.VMEM((BPX, 256), BF16),
            pltpu.VMEM((BPX, 256), BF16),
            pltpu.VMEM((2, 32, 128), F32),
            pltpu.VMEM((2, ROWS, 128), F32),
            pltpu.VMEM((4, WIDE), F32),
            pltpu.VMEM((NY * NZ, 2, 128), F32),
            pltpu.VMEM((NY - 1, NZ, 2, 128), F32),
            pltpu.VMEM((NZ, 2, 128), F32),
            pltpu.VMEM((NZ - 1, 2, 128), F32),
            pltpu.VMEM((4, WIDE), BF16),
            pltpu.VMEM((NLENS - 1, 4, WIDE), BF16),
            dma((3,)),
            dma((4,)),
            dma((2,)),
            pltpu.SemaphoreType.REGULAR,
            dma((NY - 1,)),
            dma((NY - 1,)),
            dma((NZ - 1,)),
            dma((NZ - 1,)),
            dma((NLENS - 1, len(CHUNKS))),
            dma((NLENS - 1, len(CHUNKS))),
        ],
        compiler_params=pltpu.CompilerParams(collective_id=0, has_side_effects=True),
        name="shear_step",
    )(
        patch_cycle.reshape(1, K_DEV),
        patch_block.reshape(1, K_DEV),
        m_values.reshape(1, 128),
        shell_weight,
        patches,
        legendre_panel,
        spin2_panel,
    )
    return pl.pallas_call(
        finish,
        out_shape=(shape, shape),
        in_specs=[vmem],
        out_specs=(vmem, vmem),
        name="finish",
    )(raw)


def solution(mesh):
    placed = (
        P(("sim", "lens"), None, None),
        P(("sim", "lens"), None),
        P(("sim", "lens")),
        P(),
        P(),
        P("sim", "lens", None),
        P("sim", "lens", None),
    )
    return jax.shard_map(
        on_device,
        mesh=mesh,
        in_specs=placed,
        out_specs=(P("sim", None, "lens"), P("sim", None, "lens")),
        check_vma=False,
    )
```

```python
import math

import jax
import jax.numpy as jnp
from jax import lax
from jax.experimental import pallas as pl
from jax.experimental.pallas import tpu as pltpu
from jax.sharding import PartitionSpec as P

NPIX = 16384
BPX = 2048
LMAX = 8192
SHELLS = 2
NZ = 16
NY = 4
NLENS = 8
K_DEV = 128
ROWS = K_DEV * SHELLS
BLOCK = 128
HALF = 33
WIDE = HALF * BLOCK
CHUNKS = ((0, 12), (12, 24), (24, 33))
NH = NZ // 2
HUB = NH // 2
FAR_FIRST = (0, 1, 7, 2, 6, 3, 5, 4)
MESH = pl.DeviceIdType.MESH
F32 = jnp.float32
BF16 = jnp.bfloat16


def split(value):
    high = value.astype(BF16)
    return high, (value - high.astype(F32)).astype(BF16)


def mxu(a, b):
    return jnp.dot(a, b, preferred_element_type=F32)


def cos_sin(index):
    quarter = (index + 4096) >> 13
    t = (index - (quarter << 13)).astype(F32) * (2.0 * math.pi / 32768)
    t2 = t * t
    c = 1.0 + t2 * (-0.5 + t2 * (1 / 24 + t2 * (-1 / 720 + t2 * (1 / 40320))))
    s = t * (1.0 + t2 * (-1 / 6 + t2 * (1 / 120 + t2 * (-1 / 5040 + t2 * (1 / 362880)))))
    odd = (quarter & 1) == 1
    cosine = jnp.where(odd, s, c)
    sine = jnp.where(odd, c, s)
    cosine = jnp.where(((quarter + 1) & 2) == 2, -cosine, cosine)
    sine = jnp.where((quarter & 2) == 2, -sine, sine)
    return cosine, sine


def iota(shape, dim):
    return lax.broadcasted_iota(jnp.int32, shape, dim)


def kernel(
    cycle_hbm, block_hbm, m_hbm, weight_hbm, x_hbm, l_hbm, s_hbm,
    raw,
    small, weight, xv, lv, sv, lc, sc, table_hi, table_lo, base, turn, factor,
    part, recv_y, summed, recv_z, recv_x, kpart, recv_k,
    small_sem, x_sem, panel_sem, far, met,
    send_y, got_y, send_z, got_z, send_x, got_x, send_k, got_k,
):
    sim = lax.axis_index("sim")
    lens = lax.axis_index("lens")
    z = sim // NY
    y = sim % NY

    def sim_id(z_to, y_to):
        return (z_to * NY + y_to, lens)

    barrier = pltpu.get_barrier_semaphore()
    half = z // NH
    across = (1 - half) * NH
    own = half * NH
    place = z % NH
    for d in range(1, NY):
        pl.semaphore_signal(
            barrier, inc=1, device_id=sim_id(z, (y + d) % NY), device_id_type=MESH
        )
    for d in range(1, NLENS):
        pl.semaphore_signal(
            barrier, inc=1, device_id=(sim, (lens + d) % NLENS), device_id_type=MESH
        )

    @pl.when(place != HUB)
    def _():
        pl.semaphore_signal(barrier, inc=1, device_id=sim_id(own + HUB, y), device_id_type=MESH)

    @pl.when(half == 0)
    def _():
        for e in range(NH):
            for dy in range(NY):
                pl.semaphore_signal(
                    barrier,
                    inc=1,
                    device_id=sim_id(NH + (place + e) % NH, (y + dy) % NY),
                    device_id_type=MESH,
                )


    small_copies = [
        pltpu.make_async_copy(source, small.at[i], small_sem.at[i])
        for i, source in enumerate((cycle_hbm, block_hbm, m_hbm))
    ]
    small_copies.append(pltpu.make_async_copy(weight_hbm, weight, small_sem.at[3]))
    for copy in small_copies:
        copy.start()
    x_copies = [
        pltpu.make_async_copy(
            x_hbm.at[:, :, pl.ds(512 * i, 512)], xv.at[:, :, pl.ds(512 * i, 512)], x_sem.at[i]
        )
        for i in range(4)
    ]
    for copy in x_copies:
        copy.start()
    l_copy = pltpu.make_async_copy(l_hbm, lv, panel_sem.at[0])
    s_copy = pltpu.make_async_copy(s_hbm, sv, panel_sem.at[1])
    for copy in small_copies:
        copy.wait()

    cycle_row = small[0]
    block_row = small[1]
    m_row = jnp.broadcast_to(small[2], (8, 128))
    row = iota((128, 128), 0)
    column = iota((128, 128), 1)
    slot = 8 * (column & 15) + 2 * ((column >> 4) & 3) + (column >> 6)
    permute = (row == slot).astype(BF16)
    m_high = mxu((m_row >> 6).astype(F32).astype(BF16), permute)
    m_low = mxu((m_row & 63).astype(F32).astype(BF16), permute)
    orders = (m_high * 64.0 + m_low).astype(jnp.int32)[0:1]

    a_cos, a_sin = cos_sin((128 * iota((32, 128), 0) * orders) & 32767)
    base[0, 0:32] = a_cos
    base[1, 0:32] = a_sin
    b_cos, b_sin = cos_sin((2 * iota((64, 128), 0) * orders) & 32767)

    def fill(a, carry):
        ca = base[0, pl.ds(a, 1), :]
        sa = base[1, pl.ds(a, 1), :]
        rows = pl.ds(pl.multiple_of(a * 64, 64), 64)
        c_high, c_low = split(ca * b_cos - sa * b_sin)
        s_high, s_low = split(sa * b_cos + ca * b_sin)
        table_hi[rows, 0:128] = c_high
        table_hi[rows, 128:256] = s_high
        table_lo[rows, 0:128] = c_low
        table_lo[rows, 128:256] = s_low
        return carry

    lax.fori_loop(0, 32, fill, 0)

    code = (block_row * 64 + cycle_row).astype(F32)
    row2 = iota((ROWS, 128), 0)
    picked = jnp.where(iota((ROWS, 128), 1) == (row2 >> 1), code, 0.0)
    code_column = jnp.sum(picked, axis=1, keepdims=True).astype(jnp.int32)
    phase = (code_column >> 6) * (2 * BPX) + (code_column & 1)
    turn_cos, turn_sin = cos_sin((phase * orders) & 32767)
    scale = 1.0 / (math.sqrt(NPIX) * math.sqrt(NZ * NY * NLENS))
    row_weight = jnp.where((row2 & 1) == 0, weight[0:1, 0:1], weight[0:1, 1:2]) * scale
    turn[0] = turn_cos * row_weight
    turn[1] = turn_sin * row_weight
    spread = (iota((128, ROWS), 0) == (iota((128, ROWS), 1) >> 1)).astype(BF16)
    cycle_wide = mxu(
        jnp.broadcast_to(cycle_row, (8, 128)).astype(F32).astype(BF16), spread
    )[0:1]
    onehot = ((iota((128, ROWS), 0) & 63).astype(F32) == cycle_wide).astype(F32).astype(BF16)

    total = jnp.zeros((ROWS, 256), F32)
    for i in range(8):
        if i % 2 == 0:
            x_copies[i // 2].wait()
        piece = xv[:, :, 256 * i : 256 * i + 256].reshape(ROWS, 256)
        total = total + mxu(piece, table_hi[256 * i : 256 * i + 256])
        total = total + mxu(piece, table_lo[256 * i : 256 * i + 256])
    l_copy.start()
    s_copy.start()
    zc = total[:, 0:128]
    zs = total[:, 128:256]
    real = turn[0] * zc - turn[1] * zs
    imag = -(turn[1] * zc + turn[0] * zs)
    high, low = split(jnp.concatenate([real, imag], axis=1))
    gathered = mxu(onehot, high) + mxu(onehot, low)
    left = iota((64, 128), 1) < 64
    for c in range(2):
        turned = gathered[:, 128 * c : 128 * c + 128].T
        part[:, c, :] = jnp.where(left, turned[0:64], turned[64:128])

    is_hub = (place == HUB).astype(jnp.int32)
    pl.semaphore_wait(barrier, NY - 1 + NLENS - 1 + half * (NH * NY) + is_hub * (NH - 1))

    @pl.when(half == 1)
    def _():
        for e in range(NH):
            pl.semaphore_signal(
                met, inc=1, device_id=sim_id((place + e) % NH, y), device_id_type=MESH
            )

    @pl.when(place == HUB)
    def _():
        for d in range(1, NH):
            pl.semaphore_signal(
                far, inc=1, device_id=sim_id(own + (place + d) % NH, y), device_id_type=MESH
            )

    copies_x = []
    for e in FAR_FIRST:
        for dy in (2, 1, 3, 0):
            z_to, y_to = across + (place + e) % NH, (y + dy) % NY
            copies_x.append(
                pltpu.make_async_remote_copy(
                    src_ref=part.at[y_to * NZ + z_to],
                    dst_ref=recv_x.at[e * NY + dy],
                    send_sem=send_x.at[e * NY + dy],
                    recv_sem=got_x.at[e * NY + dy],
                    device_id=sim_id(z_to, y_to),
                    device_id_type=MESH,
                )
            )

    @pl.when(half == 1)
    def _():
        for copy in copies_x:
            copy.start()

    copies = []
    for d in range(1, NY):
        y_to = (y + d) % NY
        copy = pltpu.make_async_remote_copy(
            src_ref=part.at[pl.ds(y_to * NZ + own, NH)],
            dst_ref=recv_y.at[d - 1],
            send_sem=send_y.at[d - 1],
            recv_sem=got_y.at[d - 1],
            device_id=sim_id(z, y_to),
            device_id_type=MESH,
        )
        copy.start()
        copies.append(copy)

    own_order = jnp.where(iota((8, 128), 1) == 2 * sim, m_row, 0)
    first = jnp.sum((own_order >> 7).astype(F32), axis=1, keepdims=True)[0:1]
    first16 = jnp.broadcast_to(first, (16, 128))
    below = [jnp.clip(first16 - p, 0.0, 1.0) for p in range(-1, 64)]
    for copy, panel, compact in ((l_copy, lv, lc), (s_copy, sv, sc)):
        copy.wait()
        for r in range(0, 64, 16):
            last = jnp.zeros((16, BLOCK), BF16)
            for p in range(64):
                up, at = divmod(p, HALF)
                one = panel[0, r : r + 16, BLOCK * p : BLOCK * p + BLOCK]
                two = panel[1, r : r + 16, BLOCK * (63 - p) : BLOCK * (64 - p)]
                mixed = one * (1.0 - below[p + 1]).astype(BF16) + two * below[p + 1].astype(BF16)
                last = last + two * (below[p] - below[p + 1]).astype(BF16)
                compact[64 * up + r : 64 * up + r + 16, BLOCK * at : BLOCK * at + BLOCK] = mixed
            compact[64 + r : 64 + r + 16, WIDE - 2 * BLOCK : WIDE - BLOCK] = last
            compact[64 + r : 64 + r + 16, WIDE - BLOCK : WIDE] = jnp.zeros((16, BLOCK), BF16)
    first = jnp.broadcast_to(first, (4, WIDE)).astype(jnp.int32)
    position = (iota((4, WIDE), 1) >> 7) + HALF * (iota((4, WIDE), 0) >> 1)
    second = (position < first) | (position >= 64)
    block = jnp.where(position < first, 63 - position, jnp.where(position >= 64, 63 - first, position))
    ell = (BLOCK * block + (iota((4, WIDE), 1) & 127)).astype(F32)
    factor[...] = jnp.where(
        ell >= 2.0,
        jnp.sqrt((ell + 2.0) * (ell - 1.0) / jnp.maximum(ell * (ell + 1.0), 1.0)),
        0.0,
    )

    for copy in copies:
        copy.wait_recv()
    summed[...] = part[pl.ds(y * NZ + own, NH)] + recv_y[0] + (recv_y[1] + recv_y[2])
    @pl.when(place != HUB)
    def _():
        pl.semaphore_wait(far, 1)

    for d in range(1, NH):
        i_to = (place + d) % NH
        copy = pltpu.make_async_remote_copy(
            src_ref=summed.at[i_to],
            dst_ref=recv_z.at[d - 1],
            send_sem=send_z.at[d - 1],
            recv_sem=got_z.at[d - 1],
            device_id=sim_id(own + i_to, y),
            device_id_type=MESH,
        )
        copy.start()
        copies.append(copy)

    @pl.when(half == 0)
    def _():
        pl.semaphore_wait(met, NH)
        for copy in copies_x:
            copy.start()

    for copy in copies[NY - 1 :]:
        copy.wait_recv()
    modes = summed[place]
    for d in range(NH - 1):
        modes = modes + recv_z[d]
    for copy in copies_x:
        copy.wait_recv()
    for n in range(NH * NY):
        modes = modes + recv_x[n]

    side = iota((2, 128), 1) < 64
    other = pltpu.roll(modes, 64, 1)
    rows8 = jnp.concatenate(
        [
            jnp.where(side, modes, 0.0),
            jnp.where(side, 0.0, other),
            jnp.where(side, other, 0.0),
            jnp.where(side, 0.0, modes),
        ],
        axis=0,
    ).astype(BF16)
    copies_k = []
    for i, (start, end) in enumerate(CHUNKS):
        lanes = slice(BLOCK * start, BLOCK * end)
        kappa = mxu(rows8, lc[:, lanes])
        kpart[:, lanes] = jnp.where(second[:, lanes], kappa[4:8], kappa[0:4]).astype(BF16)
        window = pl.ds(BLOCK * start, BLOCK * (end - start))
        for d in range(1, NLENS):
            lens_to = (lens + d) % NLENS
            copy = pltpu.make_async_remote_copy(
                src_ref=kpart.at[:, window],
                dst_ref=recv_k.at[d - 1, :, window],
                send_sem=send_k.at[d - 1, i],
                recv_sem=got_k.at[d - 1, i],
                device_id=(sim, lens_to),
                device_id_type=MESH,
            )
            copy.start()
            copies_k.append(copy)

    out_k = jnp.zeros((8, 128), F32)
    out_s = jnp.zeros((8, 128), F32)
    contract = (((1,), (1,)), ((), ()))
    for i, (start, end) in enumerate(CHUNKS):
        lanes = slice(BLOCK * start, BLOCK * end)
        kappa = kpart[:, lanes].astype(F32)
        for d in range(NLENS - 1):
            copies_k[(NLENS - 1) * i + d].wait_recv()
            kappa = kappa + recv_k[d, :, lanes].astype(F32)
        zero = jnp.zeros_like(kappa)
        of_second = second[:, lanes]
        shear = kappa * factor[:, lanes]
        for value, panel, kind in ((kappa, lc, 0), (shear, sc, 1)):
            value8 = jnp.concatenate(
                [jnp.where(of_second, zero, value), jnp.where(of_second, value, zero)], axis=0
            )
            out = lax.dot_general(
                value8.astype(BF16), panel[:, lanes], contract, preferred_element_type=F32
            )
            if kind == 0:
                out_k = out_k + out
            else:
                out_s = out_s + out
    scale = 1.0 / math.sqrt(LMAX)
    raw[0] = out_k * scale
    raw[1] = out_s * scale
    for copy in copies + copies_x + copies_k:
        copy.wait_send()


def finish(raw, kappa_out, shear_out):
    for kind, out in ((0, kappa_out), (1, shear_out)):
        for b in range(2):
            out[b] = raw[kind, 4 * b : 4 * b + 2, 0:64] + raw[kind, 4 * b + 2 : 4 * b + 4, 64:128]


def on_device(
    patches, patch_cycle, patch_block, m_values, shell_weight, legendre_panel, spin2_panel
):
    hbm = pl.BlockSpec(memory_space=pltpu.HBM)
    vmem = pl.BlockSpec(memory_space=pltpu.VMEM)
    shape = jax.ShapeDtypeStruct((2, 2, 64), F32)
    dma = pltpu.SemaphoreType.DMA
    operands = [
        pltpu.with_memory_space_constraint(operand, pltpu.HBM)
        for operand in (
            patch_cycle.reshape(1, K_DEV),
            patch_block.reshape(1, K_DEV),
            m_values.reshape(1, 128),
            shell_weight.reshape(1, SHELLS),
            patches,
            legendre_panel,
            spin2_panel,
        )
    ]
    raw = pl.pallas_call(
        kernel,
        out_shape=jax.ShapeDtypeStruct((2, 8, 128), F32),
        in_specs=[hbm] * 7,
        out_specs=vmem,
        scratch_shapes=[
            pltpu.VMEM((3, 1, 128), jnp.int32),
            pltpu.VMEM((1, SHELLS), F32),
            pltpu.VMEM((K_DEV, SHELLS, BPX), BF16),
            pltpu.VMEM((2, 64, LMAX), BF16),
            pltpu.VMEM((2, 64, LMAX), BF16),
            pltpu.VMEM((128, WIDE), BF16),
            pltpu.VMEM((128, WIDE), BF16),
            pltpu.VMEM((BPX, 256), BF16),
            pltpu.VMEM((BPX, 256), BF16),
            pltpu.VMEM((2, 32, 128), F32),
            pltpu.VMEM((2, ROWS, 128), F32),
            pltpu.VMEM((4, WIDE), F32),
            pltpu.VMEM((NY * NZ, 2, 128), F32),
            pltpu.VMEM((NY - 1, NH, 2, 128), F32),
            pltpu.VMEM((NH, 2, 128), F32),
            pltpu.VMEM((NH - 1, 2, 128), F32),
            pltpu.VMEM((NH * NY, 2, 128), F32),
            pltpu.VMEM((4, WIDE), BF16),
            pltpu.VMEM((NLENS - 1, 4, WIDE), BF16),
            dma((4,)),
            dma((4,)),
            dma((2,)),
            pltpu.SemaphoreType.REGULAR,
            pltpu.SemaphoreType.REGULAR,
            dma((NY - 1,)),
            dma((NY - 1,)),
            dma((NH - 1,)),
            dma((NH - 1,)),
            dma((NH * NY,)),
            dma((NH * NY,)),
            dma((NLENS - 1, len(CHUNKS))),
            dma((NLENS - 1, len(CHUNKS))),
        ],
        compiler_params=pltpu.CompilerParams(collective_id=0, has_side_effects=True, vmem_limit_bytes=24 << 20),
        name="shear_step",
    )(*operands)
    return pl.pallas_call(
        finish,
        out_shape=(shape, shape),
        in_specs=[vmem],
        out_specs=(vmem, vmem),
        compiler_params=pltpu.CompilerParams(vmem_limit_bytes=1 << 20),
        name="finish",
    )(raw)


def solution(mesh):
    placed = (
        P(("sim", "lens"), None, None),
        P(("sim", "lens"), None),
        P(("sim", "lens")),
        P(),
        P(),
        P("sim", "lens", None),
        P("sim", "lens", None),
    )
    return jax.shard_map(
        on_device,
        mesh=mesh,
        in_specs=placed,
        out_specs=(P("sim", None, "lens"), P("sim", None, "lens")),
        check_vma=False,
    )
```

```python
import math

import jax
import jax.numpy as jnp
from jax import lax
from jax.experimental import pallas as pl
from jax.experimental.pallas import tpu as pltpu
from jax.sharding import PartitionSpec as P

NPIX = 16384
BPX = 2048
LMAX = 8192
SHELLS = 2
NZ = 16
NY = 4
NLENS = 8
K_DEV = 128
ROWS = K_DEV * SHELLS
BLOCK = 128
HALF = 33
WIDE = HALF * BLOCK
CHUNKS = ((0, 12), (12, 24), (24, 33))
NH = NZ // 2
HUB = NH // 2
FAR_FIRST = (0, 1, 7, 2, 6, 3, 5, 4)
MESH = pl.DeviceIdType.MESH
F32 = jnp.float32
BF16 = jnp.bfloat16


def mxu(a, b):
    return jnp.dot(a, b, preferred_element_type=F32)


def cos_sin(index):
    quarter = (index + 4096) >> 13
    t = (index - (quarter << 13)).astype(F32) * (2.0 * math.pi / 32768)
    t2 = t * t
    c = 1.0 + t2 * (-0.5 + t2 * (1 / 24 + t2 * (-1 / 720 + t2 * (1 / 40320))))
    s = t * (1.0 + t2 * (-1 / 6 + t2 * (1 / 120 + t2 * (-1 / 5040 + t2 * (1 / 362880)))))
    odd = (quarter & 1) == 1
    cosine = jnp.where(odd, s, c)
    sine = jnp.where(odd, c, s)
    cosine = jnp.where(((quarter + 1) & 2) == 2, -cosine, cosine)
    sine = jnp.where((quarter & 2) == 2, -sine, sine)
    return cosine, sine


def iota(shape, dim):
    return lax.broadcasted_iota(jnp.int32, shape, dim)


def kernel(
    cycle_hbm, block_hbm, m_hbm, weight_hbm, x_hbm, l_hbm, s_hbm,
    raw,
    small, weight, xv, lv, sv, lc, sc, table, base, turn, factor,
    staged, part, recv_y, summed, recv_z, recv_x, kpart, recv_k,
    small_sem, x_sem, panel_sem, far, met,
    send_y, got_y, send_z, got_z, send_x, got_x, send_k, got_k,
):
    sim = lax.axis_index("sim")
    lens = lax.axis_index("lens")
    z = sim // NY
    y = sim % NY

    def sim_id(z_to, y_to):
        return (z_to * NY + y_to, lens)

    small_copies = [
        pltpu.make_async_copy(source, small.at[i], small_sem.at[i])
        for i, source in enumerate((cycle_hbm, block_hbm, m_hbm))
    ]
    small_copies.append(pltpu.make_async_copy(weight_hbm, weight, small_sem.at[3]))
    for copy in small_copies:
        copy.start()
    x_copies = [
        pltpu.make_async_copy(
            x_hbm.at[:, :, pl.ds(512 * i, 512)], xv.at[:, :, pl.ds(512 * i, 512)], x_sem.at[i]
        )
        for i in range(4)
    ]
    for copy in x_copies:
        copy.start()
    barrier = pltpu.get_barrier_semaphore()
    half = z // NH
    across = (1 - half) * NH
    own = half * NH
    place = z % NH
    for d in range(1, NY):
        pl.semaphore_signal(
            barrier, inc=1, device_id=sim_id(z, (y + d) % NY), device_id_type=MESH
        )
    for d in range(1, NLENS):
        pl.semaphore_signal(
            barrier, inc=1, device_id=(sim, (lens + d) % NLENS), device_id_type=MESH
        )

    @pl.when(place != HUB)
    def _():
        pl.semaphore_signal(barrier, inc=1, device_id=sim_id(own + HUB, y), device_id_type=MESH)

    @pl.when(half == 0)
    def _():
        for e in range(NH):
            for dy in range(NY):
                pl.semaphore_signal(
                    barrier,
                    inc=1,
                    device_id=sim_id(NH + (place + e) % NH, (y + dy) % NY),
                    device_id_type=MESH,
                )


    l_copy = pltpu.make_async_copy(l_hbm, lv, panel_sem.at[0])
    s_copy = pltpu.make_async_copy(s_hbm, sv, panel_sem.at[1])
    for copy in small_copies:
        copy.wait()

    cycle_row = small[0]
    block_row = small[1]
    m_row = jnp.broadcast_to(small[2], (8, 128))
    row = iota((128, 128), 0)
    column = iota((128, 128), 1)
    slot = 8 * (column & 15) + 2 * ((column >> 4) & 3) + (column >> 6)
    permute = (row == slot).astype(BF16)
    m_high = mxu((m_row >> 6).astype(F32).astype(BF16), permute)
    m_low = mxu((m_row & 63).astype(F32).astype(BF16), permute)
    orders = (m_high * 64.0 + m_low).astype(jnp.int32)[0:1]

    a_cos, a_sin = cos_sin((128 * iota((32, 128), 0) * orders) & 32767)
    base[0, 0:32] = a_cos
    base[1, 0:32] = a_sin
    b_cos, b_sin = cos_sin((2 * iota((64, 128), 0) * orders) & 32767)

    def fill(a, carry):
        ca = base[0, pl.ds(a, 1), :]
        sa = base[1, pl.ds(a, 1), :]
        rows = pl.ds(pl.multiple_of(a * 64, 64), 64)
        table[rows, 0:128] = (ca * b_cos - sa * b_sin).astype(BF16)
        table[rows, 128:256] = (sa * b_cos + ca * b_sin).astype(BF16)
        return carry

    lax.fori_loop(0, 32, fill, 0)

    code = (block_row * 64 + cycle_row).astype(F32)
    row2 = iota((ROWS, 128), 0)
    picked = jnp.where(iota((ROWS, 128), 1) == (row2 >> 1), code, 0.0)
    code_column = jnp.sum(picked, axis=1, keepdims=True).astype(jnp.int32)
    phase = (code_column >> 6) * (2 * BPX) + (code_column & 1)
    turn_cos, turn_sin = cos_sin((phase * orders) & 32767)
    scale = 1.0 / (math.sqrt(NPIX) * math.sqrt(NZ * NY * NLENS))
    row_weight = jnp.where((row2 & 1) == 0, weight[0:1, 0:1], weight[0:1, 1:2]) * scale
    turn[0] = turn_cos * row_weight
    turn[1] = turn_sin * row_weight
    spread = (iota((128, ROWS), 0) == (iota((128, ROWS), 1) >> 1)).astype(BF16)
    cycle_wide = mxu(
        jnp.broadcast_to(cycle_row, (8, 128)).astype(F32).astype(BF16), spread
    )[0:1]
    onehot = ((iota((128, ROWS), 0) & 63).astype(F32) == cycle_wide).astype(F32).astype(BF16)

    for copy in x_copies:
        copy.wait()
    total = mxu(xv[...].reshape(ROWS, BPX), table[...])
    l_copy.start()
    s_copy.start()
    zc = total[:, 0:128]
    zs = total[:, 128:256]
    real = turn[0] * zc - turn[1] * zs
    imag = -(turn[1] * zc + turn[0] * zs)
    gathered = mxu(onehot, jnp.concatenate([real, imag], axis=1).astype(BF16))
    left = iota((64, 128), 1) < 64
    for c in range(2):
        turned = gathered[:, 128 * c : 128 * c + 128].T
        staged[:, c, :] = jnp.where(left, turned[0:64], turned[64:128])
    part[...] = staged[...].astype(BF16)

    is_hub = (place == HUB).astype(jnp.int32)
    pl.semaphore_wait(barrier, NY - 1 + NLENS - 1 + half * (NH * NY) + is_hub * (NH - 1))

    @pl.when(half == 1)
    def _():
        for e in range(NH):
            pl.semaphore_signal(
                met, inc=1, device_id=sim_id((place + e) % NH, y), device_id_type=MESH
            )

    @pl.when(place == HUB)
    def _():
        for d in range(1, NH):
            pl.semaphore_signal(
                far, inc=1, device_id=sim_id(own + (place + d) % NH, y), device_id_type=MESH
            )

    copies_x = []
    for e in FAR_FIRST:
        for dy in (2, 1, 3, 0):
            z_to, y_to = across + (place + e) % NH, (y + dy) % NY
            copies_x.append(
                pltpu.make_async_remote_copy(
                    src_ref=part.at[y_to * NZ + z_to],
                    dst_ref=recv_x.at[e * NY + dy],
                    send_sem=send_x.at[e * NY + dy],
                    recv_sem=got_x.at[e * NY + dy],
                    device_id=sim_id(z_to, y_to),
                    device_id_type=MESH,
                )
            )

    @pl.when(half == 1)
    def _():
        for copy in copies_x:
            copy.start()

    copies = []
    for d in range(1, NY):
        y_to = (y + d) % NY
        copy = pltpu.make_async_remote_copy(
            src_ref=part.at[pl.ds(y_to * NZ + own, NH)],
            dst_ref=recv_y.at[d - 1],
            send_sem=send_y.at[d - 1],
            recv_sem=got_y.at[d - 1],
            device_id=sim_id(z, y_to),
            device_id_type=MESH,
        )
        copy.start()
        copies.append(copy)

    own_order = jnp.where(iota((8, 128), 1) == 2 * sim, m_row, 0)
    first = jnp.sum((own_order >> 7).astype(F32), axis=1, keepdims=True)[0:1]
    first16 = jnp.broadcast_to(first, (16, 128))
    below = [jnp.clip(first16 - p, 0.0, 1.0) for p in range(-1, 64)]
    for copy, panel, compact in ((l_copy, lv, lc), (s_copy, sv, sc)):
        copy.wait()
        for r in range(0, 64, 16):
            last = jnp.zeros((16, BLOCK), BF16)
            for p in range(64):
                up, at = divmod(p, HALF)
                one = panel[0, r : r + 16, BLOCK * p : BLOCK * p + BLOCK]
                two = panel[1, r : r + 16, BLOCK * (63 - p) : BLOCK * (64 - p)]
                mixed = one * (1.0 - below[p + 1]).astype(BF16) + two * below[p + 1].astype(BF16)
                last = last + two * (below[p] - below[p + 1]).astype(BF16)
                compact[64 * up + r : 64 * up + r + 16, BLOCK * at : BLOCK * at + BLOCK] = mixed
            compact[64 + r : 64 + r + 16, WIDE - 2 * BLOCK : WIDE - BLOCK] = last
            compact[64 + r : 64 + r + 16, WIDE - BLOCK : WIDE] = jnp.zeros((16, BLOCK), BF16)
    first = jnp.broadcast_to(first, (4, WIDE)).astype(jnp.int32)
    position = (iota((4, WIDE), 1) >> 7) + HALF * (iota((4, WIDE), 0) >> 1)
    second = (position < first) | (position >= 64)
    block = jnp.where(position < first, 63 - position, jnp.where(position >= 64, 63 - first, position))
    ell = (BLOCK * block + (iota((4, WIDE), 1) & 127)).astype(F32)
    factor[...] = jnp.where(
        ell >= 2.0,
        jnp.sqrt((ell + 2.0) * (ell - 1.0) / jnp.maximum(ell * (ell + 1.0), 1.0)),
        0.0,
    )

    for copy in copies:
        copy.wait_recv()
    here = part[pl.ds(y * NZ + own, NH)].astype(F32) + recv_y[0].astype(F32)
    summed[...] = here + (recv_y[1].astype(F32) + recv_y[2].astype(F32))
    @pl.when(place != HUB)
    def _():
        pl.semaphore_wait(far, 1)

    for d in range(1, NH):
        i_to = (place + d) % NH
        copy = pltpu.make_async_remote_copy(
            src_ref=summed.at[i_to],
            dst_ref=recv_z.at[d - 1],
            send_sem=send_z.at[d - 1],
            recv_sem=got_z.at[d - 1],
            device_id=sim_id(own + i_to, y),
            device_id_type=MESH,
        )
        copy.start()
        copies.append(copy)

    @pl.when(half == 0)
    def _():
        pl.semaphore_wait(met, NH)
        for copy in copies_x:
            copy.start()

    for copy in copies[NY - 1 :]:
        copy.wait_recv()
    modes = summed[place]
    for d in range(NH - 1):
        modes = modes + recv_z[d]
    for copy in copies_x:
        copy.wait_recv()
    for n in range(NH * NY):
        modes = modes + recv_x[n].astype(F32)

    side = iota((2, 128), 1) < 64
    other = pltpu.roll(modes, 64, 1)
    rows8 = jnp.concatenate(
        [
            jnp.where(side, modes, 0.0),
            jnp.where(side, 0.0, other),
            jnp.where(side, other, 0.0),
            jnp.where(side, 0.0, modes),
        ],
        axis=0,
    ).astype(BF16)
    copies_k = []
    for i, (start, end) in enumerate(CHUNKS):
        lanes = slice(BLOCK * start, BLOCK * end)
        kappa = mxu(rows8, lc[:, lanes])
        kpart[:, lanes] = jnp.where(second[:, lanes], kappa[4:8], kappa[0:4]).astype(BF16)
        window = pl.ds(BLOCK * start, BLOCK * (end - start))
        for d in range(1, NLENS):
            lens_to = (lens + d) % NLENS
            copy = pltpu.make_async_remote_copy(
                src_ref=kpart.at[:, window],
                dst_ref=recv_k.at[d - 1, :, window],
                send_sem=send_k.at[d - 1, i],
                recv_sem=got_k.at[d - 1, i],
                device_id=(sim, lens_to),
                device_id_type=MESH,
            )
            copy.start()
            copies_k.append(copy)

    out_k = jnp.zeros((8, 128), F32)
    out_s = jnp.zeros((8, 128), F32)
    contract = (((1,), (1,)), ((), ()))
    for i, (start, end) in enumerate(CHUNKS):
        lanes = slice(BLOCK * start, BLOCK * end)
        kappa = kpart[:, lanes].astype(F32)
        for d in range(NLENS - 1):
            copies_k[(NLENS - 1) * i + d].wait_recv()
            kappa = kappa + recv_k[d, :, lanes].astype(F32)
        zero = jnp.zeros_like(kappa)
        of_second = second[:, lanes]
        shear = kappa * factor[:, lanes]
        for value, panel, kind in ((kappa, lc, 0), (shear, sc, 1)):
            value8 = jnp.concatenate(
                [jnp.where(of_second, zero, value), jnp.where(of_second, value, zero)], axis=0
            )
            out = lax.dot_general(
                value8.astype(BF16), panel[:, lanes], contract, preferred_element_type=F32
            )
            if kind == 0:
                out_k = out_k + out
            else:
                out_s = out_s + out
    scale = 1.0 / math.sqrt(LMAX)
    raw[0] = out_k * scale
    raw[1] = out_s * scale
    for copy in copies + copies_x + copies_k:
        copy.wait_send()


def finish(raw, kappa_out, shear_out):
    for kind, out in ((0, kappa_out), (1, shear_out)):
        for b in range(2):
            out[b] = raw[kind, 4 * b : 4 * b + 2, 0:64] + raw[kind, 4 * b + 2 : 4 * b + 4, 64:128]


def on_device(
    patches, patch_cycle, patch_block, m_values, shell_weight, legendre_panel, spin2_panel
):
    hbm = pl.BlockSpec(memory_space=pltpu.HBM)
    vmem = pl.BlockSpec(memory_space=pltpu.VMEM)
    shape = jax.ShapeDtypeStruct((2, 2, 64), F32)
    dma = pltpu.SemaphoreType.DMA
    operands = [
        pltpu.with_memory_space_constraint(operand, pltpu.HBM)
        for operand in (
            patch_cycle.reshape(1, K_DEV),
            patch_block.reshape(1, K_DEV),
            m_values.reshape(1, 128),
            shell_weight.reshape(1, SHELLS),
            patches,
            legendre_panel,
            spin2_panel,
        )
    ]
    raw = pl.pallas_call(
        kernel,
        out_shape=jax.ShapeDtypeStruct((2, 8, 128), F32),
        in_specs=[hbm] * 7,
        out_specs=vmem,
        scratch_shapes=[
            pltpu.VMEM((3, 1, 128), jnp.int32),
            pltpu.VMEM((1, SHELLS), F32),
            pltpu.VMEM((K_DEV, SHELLS, BPX), BF16),
            pltpu.VMEM((2, 64, LMAX), BF16),
            pltpu.VMEM((2, 64, LMAX), BF16),
            pltpu.VMEM((128, WIDE), BF16),
            pltpu.VMEM((128, WIDE), BF16),
            pltpu.VMEM((BPX, 256), BF16),
            pltpu.VMEM((2, 32, 128), F32),
            pltpu.VMEM((2, ROWS, 128), F32),
            pltpu.VMEM((4, WIDE), F32),
            pltpu.VMEM((NY * NZ, 2, 128), F32),
            pltpu.VMEM((NY * NZ, 2, 128), BF16),
            pltpu.VMEM((NY - 1, NH, 2, 128), BF16),
            pltpu.VMEM((NH, 2, 128), F32),
            pltpu.VMEM((NH - 1, 2, 128), F32),
            pltpu.VMEM((NH * NY, 2, 128), BF16),
            pltpu.VMEM((4, WIDE), BF16),
            pltpu.VMEM((NLENS - 1, 4, WIDE), BF16),
            dma((4,)),
            dma((4,)),
            dma((2,)),
            pltpu.SemaphoreType.REGULAR,
            pltpu.SemaphoreType.REGULAR,
            dma((NY - 1,)),
            dma((NY - 1,)),
            dma((NH - 1,)),
            dma((NH - 1,)),
            dma((NH * NY,)),
            dma((NH * NY,)),
            dma((NLENS - 1, len(CHUNKS))),
            dma((NLENS - 1, len(CHUNKS))),
        ],
        compiler_params=pltpu.CompilerParams(collective_id=0, has_side_effects=True, vmem_limit_bytes=24 << 20),
        name="shear_step",
    )(*operands)
    return pl.pallas_call(
        finish,
        out_shape=(shape, shape),
        in_specs=[vmem],
        out_specs=(vmem, vmem),
        compiler_params=pltpu.CompilerParams(vmem_limit_bytes=1 << 20),
        name="finish",
    )(raw)


def solution(mesh):
    placed = (
        P(("sim", "lens"), None, None),
        P(("sim", "lens"), None),
        P(("sim", "lens")),
        P(),
        P(),
        P("sim", "lens", None),
        P("sim", "lens", None),
    )
    return jax.shard_map(
        on_device,
        mesh=mesh,
        in_specs=placed,
        out_specs=(P("sim", None, "lens"), P("sim", None, "lens")),
        check_vma=False,
    )
```

```python
import math

import jax
import jax.numpy as jnp
from jax import lax
from jax.experimental import pallas as pl
from jax.experimental.pallas import tpu as pltpu
from jax.sharding import PartitionSpec as P

NPIX = 16384
BPX = 2048
LMAX = 8192
SHELLS = 2
NZ = 16
NY = 4
NLENS = 8
K_DEV = 128
ROWS = K_DEV * SHELLS
BLOCK = 128
HALF = 33
WIDE = HALF * BLOCK
CHUNKS = ((0, 12), (12, 24), (24, 33))
LENS_ORDER = (4, 3, 5, 2, 6, 1, 7)
NH = NZ // 2
HUB = NH // 2
MESH = pl.DeviceIdType.MESH
F32 = jnp.float32
BF16 = jnp.bfloat16


def mxu(a, b):
    return jnp.dot(a, b, preferred_element_type=F32)


def cos_sin(index):
    quarter = (index + 4096) >> 13
    t = (index - (quarter << 13)).astype(F32) * (2.0 * math.pi / 32768)
    t2 = t * t
    c = 1.0 + t2 * (-0.5 + t2 * (1 / 24 + t2 * (-1 / 720 + t2 * (1 / 40320))))
    s = t * (1.0 + t2 * (-1 / 6 + t2 * (1 / 120 + t2 * (-1 / 5040 + t2 * (1 / 362880)))))
    odd = (quarter & 1) == 1
    cosine = jnp.where(odd, s, c)
    sine = jnp.where(odd, c, s)
    cosine = jnp.where(((quarter + 1) & 2) == 2, -cosine, cosine)
    sine = jnp.where((quarter & 2) == 2, -sine, sine)
    return cosine, sine


def iota(shape, dim):
    return lax.broadcasted_iota(jnp.int32, shape, dim)


def kernel(
    cycle_hbm, block_hbm, m_hbm, weight_hbm, x_hbm, l_hbm, s_hbm,
    raw,
    small, weight, xv, lv, sv, lc, sc, table, base, turn, factor,
    part, recv_y, summed, recv_z, recv_x, kpart, recv_k,
    small_sem, x_sem, panel_sem, far, met,
    send_y, got_y, send_z, got_z, send_x, got_x, send_k, got_k,
):
    sim = lax.axis_index("sim")
    lens = lax.axis_index("lens")
    z = sim // NY
    y = sim % NY

    def sim_id(z_to, y_to):
        return (z_to * NY + y_to, lens)

    small_copies = [
        pltpu.make_async_copy(source, small.at[i], small_sem.at[i])
        for i, source in enumerate((cycle_hbm, block_hbm, m_hbm))
    ]
    small_copies.append(pltpu.make_async_copy(weight_hbm, weight, small_sem.at[3]))
    for copy in small_copies:
        copy.start()
    x_copies = [
        pltpu.make_async_copy(
            x_hbm.at[pl.ds(32 * i, 32)], xv.at[pl.ds(32 * i, 32)], x_sem.at[i]
        )
        for i in range(4)
    ]
    for copy in x_copies:
        copy.start()
    barrier = pltpu.get_barrier_semaphore()
    half = z // NH
    across = (1 - half) * NH
    own = half * NH
    place = z % NH
    for d in range(1, NY):
        pl.semaphore_signal(
            barrier, inc=1, device_id=sim_id(z, (y + d) % NY), device_id_type=MESH
        )
    for d in range(1, NLENS):
        pl.semaphore_signal(
            barrier, inc=1, device_id=(sim, (lens + d) % NLENS), device_id_type=MESH
        )

    @pl.when(place != HUB)
    def _():
        pl.semaphore_signal(barrier, inc=1, device_id=sim_id(own + HUB, y), device_id_type=MESH)

    @pl.when(half == 0)
    def _():
        for e in range(NH):
            for dy in range(NY):
                pl.semaphore_signal(
                    barrier,
                    inc=1,
                    device_id=sim_id(NH + (place + e) % NH, (y + dy) % NY),
                    device_id_type=MESH,
                )


    l_copy = pltpu.make_async_copy(l_hbm, lv, panel_sem.at[0])
    s_copy = pltpu.make_async_copy(s_hbm, sv, panel_sem.at[1])
    for copy in small_copies:
        copy.wait()

    cycle_row = small[0]
    block_row = small[1]
    m_row = jnp.broadcast_to(small[2], (8, 128))
    row = iota((128, 128), 0)
    column = iota((128, 128), 1)
    slot = 8 * (column & 15) + 2 * ((column >> 4) & 3) + (column >> 6)
    permute = (row == slot).astype(BF16)
    m_high = mxu((m_row >> 6).astype(F32).astype(BF16), permute)
    m_low = mxu((m_row & 63).astype(F32).astype(BF16), permute)
    orders = (m_high * 64.0 + m_low).astype(jnp.int32)[0:1]

    a_cos, a_sin = cos_sin((128 * iota((32, 128), 0) * orders) & 32767)
    base[0, 0:32] = a_cos
    base[1, 0:32] = a_sin
    b_cos, b_sin = cos_sin((2 * iota((64, 128), 0) * orders) & 32767)

    def fill(a, carry):
        ca = base[0, pl.ds(a, 1), :]
        sa = base[1, pl.ds(a, 1), :]
        rows = pl.ds(pl.multiple_of(a * 64, 64), 64)
        table[rows, 0:128] = (ca * b_cos - sa * b_sin).astype(BF16)
        table[rows, 128:256] = (sa * b_cos + ca * b_sin).astype(BF16)
        return carry

    lax.fori_loop(0, 32, fill, 0)

    code = (block_row * 64 + cycle_row).astype(F32)
    row2 = iota((ROWS, 128), 0)
    picked = jnp.where(iota((ROWS, 128), 1) == (row2 >> 1), code, 0.0)
    code_column = jnp.sum(picked, axis=1, keepdims=True).astype(jnp.int32)
    phase = (code_column >> 6) * (2 * BPX) + (code_column & 1)
    turn_cos, turn_sin = cos_sin((phase * orders) & 32767)
    scale = 1.0 / (math.sqrt(NPIX) * math.sqrt(NZ * NY * NLENS))
    row_weight = jnp.where((row2 & 1) == 0, weight[0:1, 0:1], weight[0:1, 1:2]) * scale
    turn[0] = turn_cos * row_weight
    turn[1] = turn_sin * row_weight
    spread = (iota((128, ROWS), 0) == (iota((128, ROWS), 1) >> 1)).astype(BF16)
    cycle_wide = mxu(
        jnp.broadcast_to(cycle_row, (8, 128)).astype(F32).astype(BF16), spread
    )[0:1]
    onehot = ((iota((128, ROWS), 0) & 63).astype(F32) == cycle_wide).astype(F32).astype(BF16)

    for copy in x_copies:
        copy.wait()
    total = mxu(xv[...].reshape(ROWS, BPX), table[...])
    l_copy.start()
    s_copy.start()
    zc = total[:, 0:128]
    zs = total[:, 128:256]
    real = turn[0] * zc - turn[1] * zs
    imag = -(turn[1] * zc + turn[0] * zs)
    gathered = mxu(onehot, jnp.concatenate([real, imag], axis=1).astype(BF16))
    left = iota((64, 128), 1) < 64
    for c in range(2):
        turned = gathered[:, 128 * c : 128 * c + 128].T
        part[:, c, :] = jnp.where(left, turned[0:64], turned[64:128])

    is_hub = (place == HUB).astype(jnp.int32)
    pl.semaphore_wait(barrier, NY - 1 + NLENS - 1 + half * (NH * NY) + is_hub * (NH - 1))

    @pl.when(half == 1)
    def _():
        for e in range(NH):
            pl.semaphore_signal(
                met, inc=1, device_id=sim_id((place + e) % NH, y), device_id_type=MESH
            )

    @pl.when(place == HUB)
    def _():
        for d in range(1, NH):
            pl.semaphore_signal(
                far, inc=1, device_id=sim_id(own + (place + d) % NH, y), device_id_type=MESH
            )

    copies_x = []
    for n in range(NH):
        for y_to in range(NY):
            at = (n - place + NH) % NH * NY + (y_to - y + NY) % NY
            copies_x.append(
                pltpu.make_async_remote_copy(
                    src_ref=part.at[y_to * NZ + across + n],
                    dst_ref=recv_x.at[at],
                    send_sem=send_x.at[at],
                    recv_sem=got_x.at[at],
                    device_id=sim_id(across + n, y_to),
                    device_id_type=MESH,
                )
            )

    @pl.when(half == 1)
    def _():
        for copy in copies_x:
            copy.start()

    copies = []
    for d in range(1, NY):
        y_to = (y + d) % NY
        copy = pltpu.make_async_remote_copy(
            src_ref=part.at[pl.ds(y_to * NZ + own, NH)],
            dst_ref=recv_y.at[d - 1],
            send_sem=send_y.at[d - 1],
            recv_sem=got_y.at[d - 1],
            device_id=sim_id(z, y_to),
            device_id_type=MESH,
        )
        copy.start()
        copies.append(copy)

    own_order = jnp.where(iota((8, 128), 1) == 2 * sim, m_row, 0)
    first = jnp.sum((own_order >> 7).astype(F32), axis=1, keepdims=True)[0:1]
    first16 = jnp.broadcast_to(first, (16, 128))
    below = [jnp.clip(first16 - p, 0.0, 1.0) for p in range(-1, 64)]
    for copy, panel, compact in ((l_copy, lv, lc), (s_copy, sv, sc)):
        copy.wait()
        for r in range(0, 64, 16):
            last = jnp.zeros((16, BLOCK), BF16)
            for p in range(64):
                up, at = divmod(p, HALF)
                one = panel[0, r : r + 16, BLOCK * p : BLOCK * p + BLOCK]
                two = panel[1, r : r + 16, BLOCK * (63 - p) : BLOCK * (64 - p)]
                mixed = one * (1.0 - below[p + 1]).astype(BF16) + two * below[p + 1].astype(BF16)
                last = last + two * (below[p] - below[p + 1]).astype(BF16)
                compact[64 * up + r : 64 * up + r + 16, BLOCK * at : BLOCK * at + BLOCK] = mixed
            compact[64 + r : 64 + r + 16, WIDE - 2 * BLOCK : WIDE - BLOCK] = last
            compact[64 + r : 64 + r + 16, WIDE - BLOCK : WIDE] = jnp.zeros((16, BLOCK), BF16)
    first = jnp.broadcast_to(first, (4, WIDE)).astype(jnp.int32)
    position = (iota((4, WIDE), 1) >> 7) + HALF * (iota((4, WIDE), 0) >> 1)
    second = (position < first) | (position >= 64)
    block = jnp.where(position < first, 63 - position, jnp.where(position >= 64, 63 - first, position))
    ell = (BLOCK * block + (iota((4, WIDE), 1) & 127)).astype(F32)
    factor[...] = jnp.where(
        ell >= 2.0,
        jnp.sqrt((ell + 2.0) * (ell - 1.0) / jnp.maximum(ell * (ell + 1.0), 1.0)),
        0.0,
    )

    for copy in copies:
        copy.wait_recv()
    here = part[pl.ds(y * NZ + own, NH)] + recv_y[0]
    summed[...] = here + (recv_y[1] + recv_y[2])
    @pl.when(place != HUB)
    def _():
        pl.semaphore_wait(far, 1)

    for d in range(1, NH):
        i_to = (place + d) % NH
        copy = pltpu.make_async_remote_copy(
            src_ref=summed.at[i_to],
            dst_ref=recv_z.at[d - 1],
            send_sem=send_z.at[d - 1],
            recv_sem=got_z.at[d - 1],
            device_id=sim_id(own + i_to, y),
            device_id_type=MESH,
        )
        copy.start()
        copies.append(copy)

    @pl.when(half == 0)
    def _():
        pl.semaphore_wait(met, NH)
        for copy in copies_x:
            copy.start()

    for copy in copies[NY - 1 :]:
        copy.wait_recv()
    modes = summed[place]
    for d in range(NH - 1):
        modes = modes + recv_z[d]
    for copy in copies_x:
        copy.wait_recv()
    pieces = [modes] + [recv_x[n] for n in range(NH * NY)]
    while len(pieces) > 1:
        pieces = [sum(pieces[n : n + 2]) for n in range(0, len(pieces), 2)]
    modes = pieces[0]

    side = iota((2, 128), 1) < 64
    other = pltpu.roll(modes, 64, 1)
    rows8 = jnp.concatenate(
        [
            jnp.where(side, modes, 0.0),
            jnp.where(side, 0.0, other),
            jnp.where(side, other, 0.0),
            jnp.where(side, 0.0, modes),
        ],
        axis=0,
    ).astype(BF16)
    copies_k = []
    for i, (start, end) in enumerate(CHUNKS):
        lanes = slice(BLOCK * start, BLOCK * end)
        kappa = mxu(rows8, lc[:, lanes])
        kpart[:, lanes] = jnp.where(second[:, lanes], kappa[4:8], kappa[0:4]).astype(BF16)
        window = pl.ds(BLOCK * start, BLOCK * (end - start))
        for d in LENS_ORDER:
            lens_to = (lens + d) % NLENS
            copy = pltpu.make_async_remote_copy(
                src_ref=kpart.at[:, window],
                dst_ref=recv_k.at[d - 1, :, window],
                send_sem=send_k.at[d - 1, i],
                recv_sem=got_k.at[d - 1, i],
                device_id=(sim, lens_to),
                device_id_type=MESH,
            )
            copy.start()
            copies_k.append(copy)

    out_k = jnp.zeros((8, 128), F32)
    out_s = jnp.zeros((8, 128), F32)
    contract = (((1,), (1,)), ((), ()))
    for i, (start, end) in enumerate(CHUNKS):
        lanes = slice(BLOCK * start, BLOCK * end)
        kappa = kpart[:, lanes].astype(F32)
        for copy in copies_k[(NLENS - 1) * i : (NLENS - 1) * (i + 1)]:
            copy.wait_recv()
        for d in range(NLENS - 1):
            kappa = kappa + recv_k[d, :, lanes].astype(F32)
        zero = jnp.zeros_like(kappa)
        of_second = second[:, lanes]
        shear = kappa * factor[:, lanes]
        for value, panel, kind in ((kappa, lc, 0), (shear, sc, 1)):
            value8 = jnp.concatenate(
                [jnp.where(of_second, zero, value), jnp.where(of_second, value, zero)], axis=0
            )
            out = lax.dot_general(
                value8.astype(BF16), panel[:, lanes], contract, preferred_element_type=F32
            )
            if kind == 0:
                out_k = out_k + out
            else:
                out_s = out_s + out
    scale = 1.0 / math.sqrt(LMAX)
    raw[0] = out_k * scale
    raw[1] = out_s * scale
    for copy in copies + copies_x + copies_k:
        copy.wait_send()


def finish(raw, kappa_out, shear_out):
    for kind, out in ((0, kappa_out), (1, shear_out)):
        for b in range(2):
            out[b] = raw[kind, 4 * b : 4 * b + 2, 0:64] + raw[kind, 4 * b + 2 : 4 * b + 4, 64:128]


def on_device(
    patches, patch_cycle, patch_block, m_values, shell_weight, legendre_panel, spin2_panel
):
    hbm = pl.BlockSpec(memory_space=pltpu.HBM)
    vmem = pl.BlockSpec(memory_space=pltpu.VMEM)
    shape = jax.ShapeDtypeStruct((2, 2, 64), F32)
    dma = pltpu.SemaphoreType.DMA
    operands = [
        pltpu.with_memory_space_constraint(operand, pltpu.HBM)
        for operand in (
            patch_cycle.reshape(1, K_DEV),
            patch_block.reshape(1, K_DEV),
            m_values.reshape(1, 128),
            shell_weight.reshape(1, SHELLS),
            patches,
            legendre_panel,
            spin2_panel,
        )
    ]
    raw = pl.pallas_call(
        kernel,
        out_shape=jax.ShapeDtypeStruct((2, 8, 128), F32),
        in_specs=[hbm] * 7,
        out_specs=vmem,
        scratch_shapes=[
            pltpu.VMEM((3, 1, 128), jnp.int32),
            pltpu.VMEM((1, SHELLS), F32),
            pltpu.VMEM((K_DEV, SHELLS, BPX), BF16),
            pltpu.VMEM((2, 64, LMAX), BF16),
            pltpu.VMEM((2, 64, LMAX), BF16),
            pltpu.VMEM((128, WIDE), BF16),
            pltpu.VMEM((128, WIDE), BF16),
            pltpu.VMEM((BPX, 256), BF16),
            pltpu.VMEM((2, 32, 128), F32),
            pltpu.VMEM((2, ROWS, 128), F32),
            pltpu.VMEM((4, WIDE), F32),
            pltpu.VMEM((NY * NZ, 2, 128), F32),
            pltpu.VMEM((NY - 1, NH, 2, 128), F32),
            pltpu.VMEM((NH, 2, 128), F32),
            pltpu.VMEM((NH - 1, 2, 128), F32),
            pltpu.VMEM((NH * NY, 2, 128), F32),
            pltpu.VMEM((4, WIDE), BF16),
            pltpu.VMEM((NLENS - 1, 4, WIDE), BF16),
            dma((4,)),
            dma((4,)),
            dma((2,)),
            pltpu.SemaphoreType.REGULAR,
            pltpu.SemaphoreType.REGULAR,
            dma((NY - 1,)),
            dma((NY - 1,)),
            dma((NH - 1,)),
            dma((NH - 1,)),
            dma((NH * NY,)),
            dma((NH * NY,)),
            dma((NLENS - 1, len(CHUNKS))),
            dma((NLENS - 1, len(CHUNKS))),
        ],
        compiler_params=pltpu.CompilerParams(collective_id=0, has_side_effects=True, vmem_limit_bytes=24 << 20),
        name="shear_step",
    )(*operands)
    return pl.pallas_call(
        finish,
        out_shape=(shape, shape),
        in_specs=[vmem],
        out_specs=(vmem, vmem),
        compiler_params=pltpu.CompilerParams(vmem_limit_bytes=1 << 20),
        name="finish",
    )(raw)


def solution(mesh):
    placed = (
        P(("sim", "lens"), None, None),
        P(("sim", "lens"), None),
        P(("sim", "lens")),
        P(),
        P(),
        P("sim", "lens", None),
        P("sim", "lens", None),
    )
    return jax.shard_map(
        on_device,
        mesh=mesh,
        in_specs=placed,
        out_specs=(P("sim", None, "lens"), P("sim", None, "lens")),
        check_vma=False,
    )
```

```python
import math

import jax
import jax.numpy as jnp
from jax import lax
from jax.experimental import pallas as pl
from jax.experimental.pallas import tpu as pltpu
from jax.sharding import PartitionSpec as P

NPIX = 16384
BPX = 2048
LMAX = 8192
SHELLS = 2
NZ = 16
NY = 4
NLENS = 8
K_DEV = 128
ROWS = K_DEV * SHELLS
BLOCK = 128
HALF = 33
WIDE = HALF * BLOCK
CHUNKS = ((0, 14), (14, 28), (28, 33))
LENS_ORDER = (4, 3, 5, 2, 6, 1, 7)
NH = NZ // 2
HUB = NH // 2
MESH = pl.DeviceIdType.MESH
F32 = jnp.float32
BF16 = jnp.bfloat16


def mxu(a, b):
    return jnp.dot(a, b, preferred_element_type=F32)


def cos_sin(index):
    quarter = (index + 4096) >> 13
    t = (index - (quarter << 13)).astype(F32) * (2.0 * math.pi / 32768)
    t2 = t * t
    c = 1.0 + t2 * (-0.5 + t2 * (1 / 24 + t2 * (-1 / 720 + t2 * (1 / 40320))))
    s = t * (1.0 + t2 * (-1 / 6 + t2 * (1 / 120 + t2 * (-1 / 5040 + t2 * (1 / 362880)))))
    odd = (quarter & 1) == 1
    cosine = jnp.where(odd, s, c)
    sine = jnp.where(odd, c, s)
    cosine = jnp.where(((quarter + 1) & 2) == 2, -cosine, cosine)
    sine = jnp.where((quarter & 2) == 2, -sine, sine)
    return cosine, sine


def iota(shape, dim):
    return lax.broadcasted_iota(jnp.int32, shape, dim)


def kernel(
    cycle_hbm, block_hbm, m_hbm, weight_hbm, x_hbm, l_hbm, s_hbm,
    raw,
    small, weight, xv, lv, sv, lc, sc, table, base, turn, factor,
    part, recv_y, summed, recv_z, recv_x, kpart, recv_k,
    small_sem, x_sem, panel_sem, far, met,
    send_y, got_y, send_z, got_z, send_x, got_x, send_k, got_k,
):
    sim = lax.axis_index("sim")
    lens = lax.axis_index("lens")
    z = sim // NY
    y = sim % NY

    def sim_id(z_to, y_to):
        return (z_to * NY + y_to, lens)

    small_copies = [
        pltpu.make_async_copy(source, small.at[i], small_sem.at[i])
        for i, source in enumerate((cycle_hbm, block_hbm, m_hbm))
    ]
    small_copies.append(pltpu.make_async_copy(weight_hbm, weight, small_sem.at[3]))
    for copy in small_copies:
        copy.start()
    x_copies = [
        pltpu.make_async_copy(
            x_hbm.at[pl.ds(32 * i, 32)], xv.at[pl.ds(32 * i, 32)], x_sem.at[i]
        )
        for i in range(4)
    ]
    for copy in x_copies:
        copy.start()
    barrier = pltpu.get_barrier_semaphore()
    half = z // NH
    across = (1 - half) * NH
    own = half * NH
    place = z % NH
    for d in range(1, NY):
        pl.semaphore_signal(
            barrier, inc=1, device_id=sim_id(z, (y + d) % NY), device_id_type=MESH
        )
    for d in range(1, NLENS):
        pl.semaphore_signal(
            barrier, inc=1, device_id=(sim, (lens + d) % NLENS), device_id_type=MESH
        )

    @pl.when(place != HUB)
    def _():
        pl.semaphore_signal(barrier, inc=1, device_id=sim_id(own + HUB, y), device_id_type=MESH)

    @pl.when(half == 0)
    def _():
        for e in range(NH):
            for dy in range(NY):
                pl.semaphore_signal(
                    barrier,
                    inc=1,
                    device_id=sim_id(NH + (place + e) % NH, (y + dy) % NY),
                    device_id_type=MESH,
                )


    l_copy = pltpu.make_async_copy(l_hbm, lv, panel_sem.at[0])
    s_copy = pltpu.make_async_copy(s_hbm, sv, panel_sem.at[1])
    for copy in small_copies:
        copy.wait()

    cycle_row = small[0]
    block_row = small[1]
    m_row = jnp.broadcast_to(small[2], (8, 128))
    row = iota((128, 128), 0)
    column = iota((128, 128), 1)
    slot = 8 * (column & 15) + 2 * ((column >> 4) & 3) + (column >> 6)
    permute = (row == slot).astype(BF16)
    m_high = mxu((m_row >> 6).astype(F32).astype(BF16), permute)
    m_low = mxu((m_row & 63).astype(F32).astype(BF16), permute)
    orders = (m_high * 64.0 + m_low).astype(jnp.int32)[0:1]

    a_cos, a_sin = cos_sin((128 * iota((32, 128), 0) * orders) & 32767)
    base[0, 0:32] = a_cos
    base[1, 0:32] = a_sin
    b_cos, b_sin = cos_sin((2 * iota((64, 128), 0) * orders) & 32767)

    def fill(a, carry):
        ca = base[0, pl.ds(a, 1), :]
        sa = base[1, pl.ds(a, 1), :]
        rows = pl.ds(pl.multiple_of(a * 64, 64), 64)
        table[rows, 0:128] = (ca * b_cos - sa * b_sin).astype(BF16)
        table[rows, 128:256] = (sa * b_cos + ca * b_sin).astype(BF16)
        return carry

    lax.fori_loop(0, 32, fill, 0)

    code = (block_row * 64 + cycle_row).astype(F32)
    row2 = iota((ROWS, 128), 0)
    picked = jnp.where(iota((ROWS, 128), 1) == (row2 >> 1), code, 0.0)
    code_column = jnp.sum(picked, axis=1, keepdims=True).astype(jnp.int32)
    phase = (code_column >> 6) * (2 * BPX) + (code_column & 1)
    turn_cos, turn_sin = cos_sin((phase * orders) & 32767)
    scale = 1.0 / (math.sqrt(NPIX) * math.sqrt(NZ * NY * NLENS))
    row_weight = jnp.where((row2 & 1) == 0, weight[0:1, 0:1], weight[0:1, 1:2]) * scale
    turn[0] = turn_cos * row_weight
    turn[1] = turn_sin * row_weight
    spread = (iota((128, ROWS), 0) == (iota((128, ROWS), 1) >> 1)).astype(BF16)
    cycle_wide = mxu(
        jnp.broadcast_to(cycle_row, (8, 128)).astype(F32).astype(BF16), spread
    )[0:1]
    onehot = ((iota((128, ROWS), 0) & 63).astype(F32) == cycle_wide).astype(F32).astype(BF16)

    for copy in x_copies:
        copy.wait()
    total = mxu(xv[...].reshape(ROWS, BPX), table[...])
    l_copy.start()
    s_copy.start()
    zc = total[:, 0:128]
    zs = total[:, 128:256]
    real = turn[0] * zc - turn[1] * zs
    imag = -(turn[1] * zc + turn[0] * zs)
    gathered = mxu(onehot, jnp.concatenate([real, imag], axis=1).astype(BF16))
    left = iota((64, 128), 1) < 64
    for c in range(2):
        turned = gathered[:, 128 * c : 128 * c + 128].T
        part[:, c, :] = jnp.where(left, turned[0:64], turned[64:128])

    is_hub = (place == HUB).astype(jnp.int32)
    pl.semaphore_wait(barrier, NY - 1 + NLENS - 1 + half * (NH * NY) + is_hub * (NH - 1))

    copies_x = []
    for n in range(NH):
        for y_to in range(NY):
            at = (n - place + NH) % NH * NY + (y_to - y + NY) % NY
            copies_x.append(
                pltpu.make_async_remote_copy(
                    src_ref=part.at[y_to * NZ + across + n],
                    dst_ref=recv_x.at[at],
                    send_sem=send_x.at[at],
                    recv_sem=got_x.at[at],
                    device_id=sim_id(across + n, y_to),
                    device_id_type=MESH,
                )
            )

    @pl.when(half == 1)
    def _():
        for copy in copies_x:
            copy.start()

    @pl.when(half == 1)
    def _():
        for e in range(NH):
            pl.semaphore_signal(
                met, inc=1, device_id=sim_id((place + e) % NH, y), device_id_type=MESH
            )

    @pl.when(place == HUB)
    def _():
        for d in range(1, NH):
            pl.semaphore_signal(
                far, inc=1, device_id=sim_id(own + (place + d) % NH, y), device_id_type=MESH
            )

    copies = []
    for d in range(1, NY):
        y_to = (y + d) % NY
        copy = pltpu.make_async_remote_copy(
            src_ref=part.at[pl.ds(y_to * NZ + own, NH)],
            dst_ref=recv_y.at[d - 1],
            send_sem=send_y.at[d - 1],
            recv_sem=got_y.at[d - 1],
            device_id=sim_id(z, y_to),
            device_id_type=MESH,
        )
        copy.start()
        copies.append(copy)

    own_order = jnp.where(iota((8, 128), 1) == 2 * sim, m_row, 0)
    first = jnp.sum((own_order >> 7).astype(F32), axis=1, keepdims=True)[0:1]
    first16 = jnp.broadcast_to(first, (16, 128))
    below = [jnp.clip(first16 - p, 0.0, 1.0) for p in range(-1, 64)]
    for copy, panel, compact in ((l_copy, lv, lc), (s_copy, sv, sc)):
        copy.wait()
        for r in range(0, 64, 16):
            last = jnp.zeros((16, BLOCK), BF16)
            for p in range(64):
                up, at = divmod(p, HALF)
                one = panel[0, r : r + 16, BLOCK * p : BLOCK * p + BLOCK]
                two = panel[1, r : r + 16, BLOCK * (63 - p) : BLOCK * (64 - p)]
                mixed = one * (1.0 - below[p + 1]).astype(BF16) + two * below[p + 1].astype(BF16)
                last = last + two * (below[p] - below[p + 1]).astype(BF16)
                compact[64 * up + r : 64 * up + r + 16, BLOCK * at : BLOCK * at + BLOCK] = mixed
            compact[64 + r : 64 + r + 16, WIDE - 2 * BLOCK : WIDE - BLOCK] = last
            compact[64 + r : 64 + r + 16, WIDE - BLOCK : WIDE] = jnp.zeros((16, BLOCK), BF16)
    first = jnp.broadcast_to(first, (4, WIDE)).astype(jnp.int32)
    position = (iota((4, WIDE), 1) >> 7) + HALF * (iota((4, WIDE), 0) >> 1)
    second = (position < first) | (position >= 64)
    block = jnp.where(position < first, 63 - position, jnp.where(position >= 64, 63 - first, position))
    ell = (BLOCK * block + (iota((4, WIDE), 1) & 127)).astype(F32)
    factor[...] = jnp.where(
        ell >= 2.0,
        jnp.sqrt((ell + 2.0) * (ell - 1.0) / jnp.maximum(ell * (ell + 1.0), 1.0)),
        0.0,
    )

    for copy in copies:
        copy.wait_recv()
    here = part[pl.ds(y * NZ + own, NH)] + recv_y[0]
    summed[...] = here + (recv_y[1] + recv_y[2])
    @pl.when(place != HUB)
    def _():
        pl.semaphore_wait(far, 1)

    for d in range(1, NH):
        i_to = (place + d) % NH
        copy = pltpu.make_async_remote_copy(
            src_ref=summed.at[i_to],
            dst_ref=recv_z.at[d - 1],
            send_sem=send_z.at[d - 1],
            recv_sem=got_z.at[d - 1],
            device_id=sim_id(own + i_to, y),
            device_id_type=MESH,
        )
        copy.start()
        copies.append(copy)

    @pl.when(half == 0)
    def _():
        pl.semaphore_wait(met, NH)
        for copy in copies_x:
            copy.start()

    for copy in copies[NY - 1 :]:
        copy.wait_recv()
    modes = summed[place]
    for d in range(NH - 1):
        modes = modes + recv_z[d]
    for copy in copies_x:
        copy.wait_recv()
    pieces = [modes] + [recv_x[n] for n in range(NH * NY)]
    while len(pieces) > 1:
        pieces = [sum(pieces[n : n + 2]) for n in range(0, len(pieces), 2)]
    modes = pieces[0]

    side = iota((2, 128), 1) < 64
    other = pltpu.roll(modes, 64, 1)
    rows8 = jnp.concatenate(
        [
            jnp.where(side, modes, 0.0),
            jnp.where(side, 0.0, other),
            jnp.where(side, other, 0.0),
            jnp.where(side, 0.0, modes),
        ],
        axis=0,
    ).astype(BF16)
    copies_k = []
    for i, (start, end) in enumerate(CHUNKS):
        lanes = slice(BLOCK * start, BLOCK * end)
        kappa = mxu(rows8, lc[:, lanes])
        kpart[:, lanes] = jnp.where(second[:, lanes], kappa[4:8], kappa[0:4]).astype(BF16)
        window = pl.ds(BLOCK * start, BLOCK * (end - start))
        for d in LENS_ORDER:
            lens_to = (lens + d) % NLENS
            copy = pltpu.make_async_remote_copy(
                src_ref=kpart.at[:, window],
                dst_ref=recv_k.at[d - 1, :, window],
                send_sem=send_k.at[d - 1, i],
                recv_sem=got_k.at[d - 1, i],
                device_id=(sim, lens_to),
                device_id_type=MESH,
            )
            copy.start()
            copies_k.append(copy)

    out_k = jnp.zeros((8, 128), F32)
    out_s = jnp.zeros((8, 128), F32)
    contract = (((1,), (1,)), ((), ()))
    for i, (start, end) in enumerate(CHUNKS):
        lanes = slice(BLOCK * start, BLOCK * end)
        kappa = kpart[:, lanes].astype(F32)
        for copy in copies_k[(NLENS - 1) * i : (NLENS - 1) * (i + 1)]:
            copy.wait_recv()
        for d in range(NLENS - 1):
            kappa = kappa + recv_k[d, :, lanes].astype(F32)
        zero = jnp.zeros_like(kappa)
        of_second = second[:, lanes]
        shear = kappa * factor[:, lanes]
        for value, panel, kind in ((kappa, lc, 0), (shear, sc, 1)):
            value8 = jnp.concatenate(
                [jnp.where(of_second, zero, value), jnp.where(of_second, value, zero)], axis=0
            )
            out = lax.dot_general(
                value8.astype(BF16), panel[:, lanes], contract, preferred_element_type=F32
            )
            if kind == 0:
                out_k = out_k + out
            else:
                out_s = out_s + out
    scale = 1.0 / math.sqrt(LMAX)
    raw[0] = out_k * scale
    raw[1] = out_s * scale
    for copy in copies + copies_x + copies_k:
        copy.wait_send()


def finish(raw, kappa_out, shear_out):
    for kind, out in ((0, kappa_out), (1, shear_out)):
        for b in range(2):
            out[b] = raw[kind, 4 * b : 4 * b + 2, 0:64] + raw[kind, 4 * b + 2 : 4 * b + 4, 64:128]


def on_device(
    patches, patch_cycle, patch_block, m_values, shell_weight, legendre_panel, spin2_panel
):
    hbm = pl.BlockSpec(memory_space=pltpu.HBM)
    vmem = pl.BlockSpec(memory_space=pltpu.VMEM)
    shape = jax.ShapeDtypeStruct((2, 2, 64), F32)
    dma = pltpu.SemaphoreType.DMA
    operands = [
        pltpu.with_memory_space_constraint(operand, pltpu.HBM)
        for operand in (
            patch_cycle.reshape(1, K_DEV),
            patch_block.reshape(1, K_DEV),
            m_values.reshape(1, 128),
            shell_weight.reshape(1, SHELLS),
            patches,
            legendre_panel,
            spin2_panel,
        )
    ]
    raw = pl.pallas_call(
        kernel,
        out_shape=jax.ShapeDtypeStruct((2, 8, 128), F32),
        in_specs=[hbm] * 7,
        out_specs=vmem,
        scratch_shapes=[
            pltpu.VMEM((3, 1, 128), jnp.int32),
            pltpu.VMEM((1, SHELLS), F32),
            pltpu.VMEM((K_DEV, SHELLS, BPX), BF16),
            pltpu.VMEM((2, 64, LMAX), BF16),
            pltpu.VMEM((2, 64, LMAX), BF16),
            pltpu.VMEM((128, WIDE), BF16),
            pltpu.VMEM((128, WIDE), BF16),
            pltpu.VMEM((BPX, 256), BF16),
            pltpu.VMEM((2, 32, 128), F32),
            pltpu.VMEM((2, ROWS, 128), F32),
            pltpu.VMEM((4, WIDE), F32),
            pltpu.VMEM((NY * NZ, 2, 128), F32),
            pltpu.VMEM((NY - 1, NH, 2, 128), F32),
            pltpu.VMEM((NH, 2, 128), F32),
            pltpu.VMEM((NH - 1, 2, 128), F32),
            pltpu.VMEM((NH * NY, 2, 128), F32),
            pltpu.VMEM((4, WIDE), BF16),
            pltpu.VMEM((NLENS - 1, 4, WIDE), BF16),
            dma((4,)),
            dma((4,)),
            dma((2,)),
            pltpu.SemaphoreType.REGULAR,
            pltpu.SemaphoreType.REGULAR,
            dma((NY - 1,)),
            dma((NY - 1,)),
            dma((NH - 1,)),
            dma((NH - 1,)),
            dma((NH * NY,)),
            dma((NH * NY,)),
            dma((NLENS - 1, len(CHUNKS))),
            dma((NLENS - 1, len(CHUNKS))),
        ],
        compiler_params=pltpu.CompilerParams(collective_id=0, has_side_effects=True, vmem_limit_bytes=24 << 20),
        name="shear_step",
    )(*operands)
    return pl.pallas_call(
        finish,
        out_shape=(shape, shape),
        in_specs=[vmem],
        out_specs=(vmem, vmem),
        compiler_params=pltpu.CompilerParams(vmem_limit_bytes=1 << 20),
        name="finish",
    )(raw)


def solution(mesh):
    placed = (
        P(("sim", "lens"), None, None),
        P(("sim", "lens"), None),
        P(("sim", "lens")),
        P(),
        P(),
        P("sim", "lens", None),
        P("sim", "lens", None),
    )
    return jax.shard_map(
        on_device,
        mesh=mesh,
        in_specs=placed,
        out_specs=(P("sim", None, "lens"), P("sim", None, "lens")),
        check_vma=False,
    )
```
